256 devices in a mesh: seq: 64 (over x_hi, y, z), head: 4 (over x_lo, core).
Axes of the slice: x: 4 (x_hi: 2, x_lo: 2; x = x_hi * 2 + x_lo), y: 4, z: 8, core: 2. Of those that a mesh axis runs over, the one named last changes fastest.
Arguments:
- queries: bfloat16 [98304, 2048], P('seq', 'head'), may hold values from -200 to 200
- keys_values: bfloat16 [2, 98304, 2048], P(None, 'seq', 'head'), may hold values from -6 to 6
- global_ids: int32 [2], replicated, may hold values from 0 to 1535
- rand_ids: int32 [1536, 3], replicated, may hold values from 0 to 1535, as said below
- out_weight: bfloat16 [2048, 4096], P(None, 'head'), may hold values from -2 to 2
Outputs:
- projected: bfloat16 [98304, 4096], P('seq', 'head')
The draws below stay inside these ranges and needn't reach their ends.
Inputs may be any that keep to these rules, and one draw needn't show every extreme that they name: `rand_ids`: row i lists the 3 random key blocks of query block i. Among the 24 rows of one seq shard, at most 2 listed blocks lie on any one shard, and at most 1 of one column do; both bounds are reached.
All inputs are finite; a program needn't handle non-finite values.
Results may differ from the reference program's by a relative error of at most 0.0057.
Values may be sent and summed in bfloat16 or wider, within the bound.
A program may use at most 128 MiB of HBM per device.

```python
import jax
import jax.numpy as jnp
from jax import lax

D = 4096
HEADS = 16
HEAD_DIM = 128
BLOCK = 64
NGLOBAL = 2
NRANDOM = 3
BLOCKS_DEV = 24
NBLOCKS = 1536
TOKENS = 98304


def key_field(key):
    return jax.random.truncated_normal(jax.random.fold_in(key, 11), -6.0, 6.0, (TOKENS, HEADS * HEAD_DIM), jnp.float32)


def draw_keys_values(key, part):
    keys = key_field(key)
    values = jax.random.truncated_normal(jax.random.fold_in(key, 12), -6.0, 6.0, (TOKENS, HEADS * HEAD_DIM), jnp.float32)
    return jnp.stack([keys, values]).astype(jnp.bfloat16)


def draw_queries(key, part):
    base = jax.random.truncated_normal(jax.random.fold_in(key, 13), -6.0, 6.0, (TOKENS, HEADS * HEAD_DIM), jnp.float32)
    return base.astype(jnp.bfloat16)


def draw_rand_ids(key, part):
    shards = NBLOCKS // BLOCKS_DEV
    heat = jax.random.permutation(jax.random.fold_in(key, 21), shards)
    jitter = jax.random.randint(jax.random.fold_in(key, 22), (shards, shards), 0, max(shards // 4, 1) + 1)
    scores = (heat[None, :] + jitter) * shards + jnp.arange(shards)[None, :]
    ordering = jnp.argsort(scores, axis=1, stable=True)
    position = (jnp.arange(BLOCKS_DEV)[None, :] + BLOCKS_DEV * jnp.arange(NRANDOM)[:, None]) % shards
    sources = ordering[:, position]
    offsets = jax.random.randint(jax.random.fold_in(key, 23), (shards, NRANDOM, BLOCKS_DEV), 0, BLOCKS_DEV)
    listed = sources * BLOCKS_DEV + offsets
    return jnp.transpose(listed, (0, 2, 1)).reshape(NBLOCKS, NRANDOM).astype(jnp.int32)


def block_scale(stream_key, dims, cuts, least, high):
    def one(dim, shards_of):
        steps = jax.random.uniform(jax.random.fold_in(jax.random.fold_in(stream_key, 6), dim), (shards_of,), jnp.float32, least / len(cuts), high / len(cuts))
        return jnp.repeat(jnp.exp(steps), dims[dim] // shards_of).reshape((-1,) + (1,) * (len(dims) - dim - 1))

    level = one(*cuts[0])
    for cut in cuts[1:]:
        level = level * one(*cut)
    return level


def scatter_about(key, shape, scale, limit, split=(), held_as=jnp.bfloat16):
    loudness = block_scale(key, shape, split, -0.22, 0.18) if split else 1.0
    result = jax.random.normal(key, shape, jnp.float32) * scale * loudness
    return jnp.minimum(jnp.maximum(result, -limit), limit).astype(held_as)


def setup_inputs(seed: int = 0) -> dict:
    streams_of = jax.random.split(jax.random.key(seed), 6)
    queries = draw_queries(jax.random.fold_in(streams_of[5], 71), 0)
    keys_values = draw_keys_values(jax.random.fold_in(streams_of[5], 71), 0)
    global_ids = jax.random.randint(streams_of[2], (NGLOBAL,), 0, NBLOCKS).astype(jnp.int32)
    rand_ids = draw_rand_ids(jax.random.fold_in(streams_of[5], 71), 0)
    out_weight = scatter_about(streams_of[4], (HEADS * HEAD_DIM, D), (max(HEADS * HEAD_DIM // 256, 1)) ** -0.5, 2.0, ((1, 4),))
    return {"queries": queries, "keys_values": keys_values, "global_ids": global_ids, "rand_ids": rand_ids, "out_weight": out_weight}


group_blocks = 8


def attend_blocks(query_part, local_keys, local_values, glob_keys, glob_values, valid):
    scale = 1.0 / (HEAD_DIM ** 0.5)
    near_scores = jnp.einsum("bqhd,bkhd->bhqk", query_part, local_keys) * scale
    near_scores = jnp.where(valid[:, None, None, :], near_scores, -jnp.inf)
    glob_scores = jnp.einsum("bqhd,khd->bhqk", query_part, glob_keys) * scale
    highest = jnp.maximum(jnp.max(near_scores, axis=-1), jnp.max(glob_scores, axis=-1))
    near_exp = jnp.exp(near_scores - highest[..., None])
    glob_exp = jnp.exp(glob_scores - highest[..., None])
    total = jnp.sum(near_exp, axis=-1) + jnp.sum(glob_exp, axis=-1)
    near_weights = (near_exp / total[..., None]).astype(jnp.bfloat16).astype(jnp.float32)
    glob_weights = (glob_exp / total[..., None]).astype(jnp.bfloat16).astype(jnp.float32)
    mixed = jnp.einsum("bhqk,bkhd->bqhd", near_weights, local_values)
    mixed = mixed + jnp.einsum("bhqk,khd->bqhd", glob_weights, glob_values)
    return mixed.astype(jnp.bfloat16)


def reference(queries, keys_values, global_ids, rand_ids, out_weight):
    query_blocks = queries.reshape(NBLOCKS, BLOCK, HEADS, HEAD_DIM)
    pair_blocks = keys_values.reshape(2, NBLOCKS, BLOCK, HEADS, HEAD_DIM)
    glob = pair_blocks[:, global_ids].reshape(2, NGLOBAL * BLOCK, HEADS, HEAD_DIM).astype(jnp.float32)
    segment = jnp.arange((3 + NRANDOM) * BLOCK, dtype=jnp.int32) // BLOCK

    def one_group(first):
        block_ids = first + jnp.arange(group_blocks, dtype=jnp.int32)
        before = pair_blocks[:, jnp.clip(block_ids - 1, 0, NBLOCKS - 1)]
        current = pair_blocks[:, block_ids]
        after = pair_blocks[:, jnp.clip(block_ids + 1, 0, NBLOCKS - 1)]
        remote = pair_blocks[:, rand_ids[block_ids]].reshape(2, group_blocks, NRANDOM * BLOCK, HEADS, HEAD_DIM)
        local = jnp.concatenate([before, current, after, remote], axis=2).astype(jnp.float32)
        drop_before = (segment[None, :] == 0) & (block_ids[:, None] == 0)
        drop_after = (segment[None, :] == 2) & (block_ids[:, None] == NBLOCKS - 1)
        valid = jnp.logical_not(drop_before | drop_after)
        query_part = query_blocks[block_ids].astype(jnp.float32)
        return attend_blocks(query_part, local[0], local[1], glob[0], glob[1], valid)

    starts = jnp.arange(NBLOCKS // group_blocks, dtype=jnp.int32) * group_blocks
    attended = lax.map(one_group, starts).reshape(TOKENS, HEADS * HEAD_DIM)
    return jnp.dot(attended, out_weight, preferred_element_type=jnp.float32).astype(jnp.bfloat16)
```

```python
import functools
import math

import jax
import jax.numpy as jnp
from jax import lax
from jax.experimental import pallas as pl
from jax.experimental.pallas import tpu as pltpu
from jax.sharding import PartitionSpec as P

HEAD_DIM = 128
BLOCK = 64
NGLOBAL = 2
NRANDOM = 3
MESH = pl.DeviceIdType.MESH

NXH, NY, NZ, NXL, NC = 2, 4, 8, 2, 2
LINES = NXH * NY
SHARD_BLOCKS = 24
ROWS = SHARD_BLOCKS * BLOCK
HALF_BLOCKS = SHARD_BLOCKS // NC
HALF = HALF_BLOCKS * BLOCK
LINE_BLOCKS = NZ * SHARD_BLOCKS
Q_BLOCKS = NZ * HALF_BLOCKS


def coords():
    seq = lax.axis_index("seq")
    head = lax.axis_index("head")
    return seq // (NY * NZ), (seq // NZ) % NY, seq % NZ, head // NC, head % NC


def device(xh, y, z, xl, c):
    return ((xh * NY + y) * NZ + z, xl * NC + c)


def remote(src, dst, send_sem, recv_sem, target):
    return pltpu.make_async_remote_copy(
        src_ref=src, dst_ref=dst, send_sem=send_sem, recv_sem=recv_sem,
        device_id=target, device_id_type=MESH,
    )


def nearest(k):
    return (k % 2) * ((k + 1) // 2) - (1 - k % 2) * (k // 2)


(KX, VX0, VX1, VX2, VX3, KU, KD, VU, VD, K2U, K2D, KFU, KFD, VFU, VFD, KF2U, KF2D) = range(17)
NCLASS = 17


def gather_kernel(q_ref, kv_ref, full_ref, qr_ref, zs, zr, ss, rs, bs, br):
    xh, y, z, xl, c = coords()
    line = xh * NY + y
    up, down, opp = (y + 1) % NY, (y + NY - 1) % NY, (y + 2) % NY
    ox = 1 - xh
    to_x, to_up, to_down = device(ox, y, z, xl, c), device(xh, up, z, xl, c), device(xh, down, z, xl, c)
    to_sib = device(xh, y, z, xl, 1 - c)

    barrier = pltpu.get_barrier_semaphore()
    friends = [
        device(xh, y, (z + dz) % NZ, xl, (c + dc) % NC)
        for dz in range(NZ) for dc in range(NC) if dz or dc
    ] + [to_x, to_up, to_down]
    for friend in friends:
        pl.semaphore_signal(barrier, inc=1, device_id=friend, device_id_type=MESH)
    pl.semaphore_wait(barrier, len(friends))

    def z_parts(t, kind, half):
        cols = pl.ds(pl.multiple_of((t - 4 * c) * HEAD_DIM, HEAD_DIM), HEAD_DIM)
        rows = pl.ds(half * HALF, HALF)
        if kind == 2:
            return q_ref.at[rows, cols], qr_ref.at[z]
        return kv_ref.at[kind, rows, cols], full_ref.at[kind, line, half, z]

    def z_each(k, kinds, remote_fn, local_fn):
        t = (z + nearest(k) + NZ) % NZ

        @pl.when(t // 4 == c)
        def _():
            for kind in kinds:
                for half in range(NC):
                    src, dst = z_parts(t, kind, half)
                    mine = jnp.logical_and(t == z, c == half)
                    if local_fn is not None:
                        @pl.when(mine)
                        def _():
                            local_fn(pltpu.make_async_copy(src, dst, zr.at[kind, z]))

                    @pl.when(jnp.logical_not(mine))
                    def _():
                        remote_fn(remote(src, dst, zs.at[kind, half, k], zr.at[kind, z],
                                         device(xh, y, t, xl, half)))

    @pl.loop(0, NZ)
    def _(k):
        z_each(k, (0, 1), lambda d: d.start(), lambda d: d.start())

    @pl.loop(0, NZ)
    def _(k):
        z_each(k, (2,), lambda d: d.start(), lambda d: d.start())

    H = HALF // 2

    def part(kv, ln, p, rows=None):
        ref = full_ref.at[kv, ln, c, p]
        return ref if rows is None else ref.at[pl.ds(rows * H, H)]

    def copy(cls, k, p, kv, ln, target, rows=None):
        ref = part(kv, ln, p, rows)
        return remote(ref, ref, ss.at[cls, k], rs.at[cls, k], target)

    def got(cls, k, p, kv, ln, rows=None):
        copy(cls, k, p, kv, ln, to_x, rows).wait_recv()

    def sib(k, p, kv, ln):
        ref = full_ref.at[kv, ln, c, p]
        return remote(ref, ref, bs.at[kv, ln, k], br.at[kv, ln, k], to_sib)

    def at(xx, yy):
        return xx * NY + yy

    sent = {
        KX: (0, line, to_x, None),
        KU: (0, line, to_up, None), KD: (0, line, to_down, None),
        VU: (1, line, to_up, None), VD: (1, line, to_down, None),
        K2U: (0, at(ox, y), to_up, None), K2D: (0, at(ox, y), to_down, None),
        KFU: (0, at(xh, down), to_up, 0), KFD: (0, at(xh, up), to_down, 1),
        VFU: (1, at(xh, down), to_up, 0), VFD: (1, at(xh, up), to_down, 1),
        KF2U: (0, at(ox, down), to_up, 0), KF2D: (0, at(ox, up), to_down, 1),
        VX0: (1, line, to_x, None), VX1: (1, at(xh, down), to_x, None),
        VX2: (1, at(xh, up), to_x, None), VX3: (1, at(xh, opp), to_x, None),
    }
    received = {
        KX: (0, at(ox, y), None),
        KU: (0, at(xh, down), None), KD: (0, at(xh, up), None),
        VU: (1, at(xh, down), None), VD: (1, at(xh, up), None),
        K2U: (0, at(ox, down), None), K2D: (0, at(ox, up), None),
        KFU: (0, at(xh, opp), 0), KFD: (0, at(xh, opp), 1),
        VFU: (1, at(xh, opp), 0), VFD: (1, at(xh, opp), 1),
        KF2U: (0, at(ox, opp), 0), KF2D: (0, at(ox, opp), 1),
        VX0: (1, at(ox, y), None), VX1: (1, at(ox, down), None),
        VX2: (1, at(ox, up), None), VX3: (1, at(ox, opp), None),
    }

    def send(cls, k, p):
        kv, ln, target, rows = sent[cls]
        copy(cls, k, p, kv, ln, target, rows).start()

    def wait(cls, k, p):
        kv, ln, rows = received[cls]
        got(cls, k, p, kv, ln, rows)

    @pl.loop(0, NZ + 3)
    def _(step):
        def stage(delay, body):
            k = step - delay

            @pl.when(jnp.logical_and(k >= 0, k < NZ))
            def _():
                body(k, (z + nearest(k) + NZ) % NZ)

        def stage1(k, p):
            for kind in range(2):
                ref = full_ref.at[kind, line, c, p]
                remote(ref, ref, zs.at[kind, 0, 0], zr.at[kind, p], to_x).wait_recv()
            for cls in (KX, KU, KD, VU, VD, VX0):
                send(cls, k, p)
            sib(k, p, 0, line).start()
            sib(k, p, 1, line).start()

        def stage2(k, p):
            wait(KX, k, p)
            send(K2U, k, p)
            send(K2D, k, p)
            wait(KU, k, p)
            send(KFU, k, p)
            wait(KD, k, p)
            send(KFD, k, p)
            wait(VU, k, p)
            send(VFU, k, p)
            send(VX1, k, p)
            wait(VD, k, p)
            send(VFD, k, p)
            send(VX2, k, p)
            sib(k, p, 0, at(ox, y)).start()
            for yy in (down, up):
                sib(k, p, 0, at(xh, yy)).start()
                sib(k, p, 1, at(xh, yy)).start()

        def stage3(k, p):
            wait(K2U, k, p)
            send(KF2U, k, p)
            wait(K2D, k, p)
            send(KF2D, k, p)
            wait(VFU, k, p)
            wait(VFD, k, p)
            send(VX3, k, p)
            wait(KFU, k, p)
            wait(KFD, k, p)
            wait(VX0, k, p)
            sib(k, p, 0, at(xh, opp)).start()
            sib(k, p, 1, at(xh, opp)).start()
            sib(k, p, 0, at(ox, down)).start()
            sib(k, p, 0, at(ox, up)).start()
            sib(k, p, 1, at(ox, y)).start()

        def stage4(k, p):
            wait(KF2U, k, p)
            wait(KF2D, k, p)
            sib(k, p, 0, at(ox, opp)).start()
            for cls, yy in ((VX1, down), (VX2, up), (VX3, opp)):
                wait(cls, k, p)
                sib(k, p, 1, at(ox, yy)).start()

        stage(3, stage4)
        stage(2, stage3)
        stage(1, stage2)
        stage(0, stage1)

    @pl.loop(0, NZ)
    def _(k):
        p = (z + nearest(k) + NZ) % NZ
        remote(qr_ref.at[p], qr_ref.at[p], zs.at[2, 0, 0], zr.at[2, p], to_x).wait_recv()
        z_each(k, (0, 1, 2), lambda d: d.wait_send(), None)
        for cls in range(NCLASS):
            kv, ln, target, rows = sent[cls]
            copy(cls, k, p, kv, ln, target, rows).wait_send()

        @pl.loop(0, LINES)
        def _(ln):
            for kv in range(2):
                sib(k, p, kv, ln).wait_send()
                other = full_ref.at[kv, ln, 1 - c, p]
                remote(other, other, bs.at[kv, ln, k], br.at[kv, ln, k], to_sib).wait_recv()


def gather_call(queries, keys_values):
    anyspace = pl.BlockSpec(memory_space=pl.ANY)
    return pl.pallas_call(
        gather_kernel,
        out_shape=(
            jax.ShapeDtypeStruct((2, LINES, NC, NZ, HALF, HEAD_DIM), jnp.bfloat16),
            jax.ShapeDtypeStruct((NZ, HALF, HEAD_DIM), jnp.bfloat16),
        ),
        in_specs=[anyspace, anyspace],
        out_specs=(anyspace, anyspace),
        scratch_shapes=[
            pltpu.SemaphoreType.DMA((3, NC, NZ)),
            pltpu.SemaphoreType.DMA((3, NZ)),
            pltpu.SemaphoreType.DMA((NCLASS, NZ)),
            pltpu.SemaphoreType.DMA((NCLASS, NZ)),
            pltpu.SemaphoreType.DMA((2, LINES, NZ)),
            pltpu.SemaphoreType.DMA((2, LINES, NZ)),
        ],
        compiler_params=pltpu.CompilerParams(collective_id=1, has_side_effects=True),
        name="gather_keys_values",
    )(queries, keys_values)


AHEAD = 16
SCALE = math.log2(math.e) / HEAD_DIM**0.5


def attend_kernel(meta, rand, q_ref, full_ref, o_ref, near, glob, far, near_sem, edge_sem, glob_sem, far_sem):
    line, c = meta[0], meta[1]

    def near_copy(kv, zz, half):
        src = full_ref.at[kv, pl.ds(((line * NC + half) * NZ + zz) * HALF_BLOCKS, HALF_BLOCKS)]
        dst = near.at[kv, pl.ds(1 + zz * SHARD_BLOCKS + half * HALF_BLOCKS, HALF_BLOCKS)]
        return pltpu.make_async_copy(src, dst, near_sem.at[kv, zz, half])

    def edge_copy(kv, side):
        return pltpu.make_async_copy(
            full_ref.at[kv, meta[2 + side]], near.at[kv, side * (LINE_BLOCKS + 1)], edge_sem.at[kv, side]
        )

    def glob_copy(kv, g):
        return pltpu.make_async_copy(full_ref.at[kv, meta[4 + g]], glob.at[kv, g], glob_sem.at[kv, g])

    def far_start(n):
        for kv in range(2):
            for r in range(NRANDOM):
                pltpu.make_async_copy(
                    full_ref.at[kv, rand[n * NRANDOM + r]], far.at[n, kv, r], far_sem.at[n]
                ).start()

    for kv in range(2):
        for i in range(2):
            glob_copy(kv, i).start()
            edge_copy(kv, i).start()

    @pl.loop(0, NZ)
    def _(zz):
        for kv in range(2):
            for half in range(NC):
                near_copy(kv, zz, half).start()

    @pl.loop(0, AHEAD)
    def _(n):
        far_start(n)

    for kv in range(2):
        for i in range(2):
            glob_copy(kv, i).wait()
            edge_copy(kv, i).wait()

    @pl.loop(0, NZ)
    def _(zz):
        for kv in range(2):
            for half in range(NC):
                near_copy(kv, zz, half).wait()

    column = lax.broadcasted_iota(jnp.int32, (1, 512), 1)

    def one(n):
        pltpu.make_async_copy(far.at[n], far.at[n], far_sem.at[n]).wait()

        @pl.when(n + AHEAD < Q_BLOCKS)
        def _():
            far_start(n + AHEAD)

        middle = (n // HALF_BLOCKS) * SHARD_BLOCKS + c * HALF_BLOCKS + n % HALF_BLOCKS
        block = line * LINE_BLOCKS + middle
        first = jnp.logical_and(block == 0, column < BLOCK)
        last = jnp.logical_and(
            block == LINES * LINE_BLOCKS - 1, jnp.logical_and(column >= 2 * BLOCK, column < 3 * BLOCK)
        )
        bias = jnp.where(jnp.logical_or(first, last), -jnp.inf, 0.0).astype(jnp.float32)

        def listed(kv):
            return jnp.concatenate(
                [
                    near[kv, pl.ds(middle, 3)].reshape(3 * BLOCK, HEAD_DIM),
                    far[n, kv].reshape(NRANDOM * BLOCK, HEAD_DIM),
                    glob[kv].reshape(NGLOBAL * BLOCK, HEAD_DIM),
                ],
                axis=0,
            )

        scores = lax.dot_general(
            q_ref[n], listed(0), (((1,), (1,)), ((), ())), preferred_element_type=jnp.float32
        )
        scores = scores * SCALE + bias
        highest = jnp.max(scores, axis=1, keepdims=True)
        weights = jnp.exp2(scores - highest)
        total = jnp.sum(weights, axis=1, keepdims=True)
        mixed = jnp.dot(weights.astype(jnp.bfloat16), listed(1), preferred_element_type=jnp.float32)
        o_ref[n] = (mixed / total).astype(jnp.bfloat16)

    @pl.loop(0, Q_BLOCKS // 4)
    def _(m):
        for u in range(4):
            one(m * 4 + u)


def attend_call(meta, rand, q, full):
    whole = pl.BlockSpec(memory_space=pltpu.VMEM)
    smem = pl.BlockSpec(memory_space=pltpu.SMEM)
    return pl.pallas_call(
        attend_kernel,
        out_shape=jax.ShapeDtypeStruct((Q_BLOCKS, BLOCK, HEAD_DIM), jnp.bfloat16),
        in_specs=[smem, smem, whole, pl.BlockSpec(memory_space=pl.ANY)],
        out_specs=whole,
        scratch_shapes=[
            pltpu.VMEM((2, LINE_BLOCKS + 2, BLOCK, HEAD_DIM), jnp.bfloat16),
            pltpu.VMEM((2, NGLOBAL, BLOCK, HEAD_DIM), jnp.bfloat16),
            pltpu.VMEM((Q_BLOCKS, 2, NRANDOM, BLOCK, HEAD_DIM), jnp.bfloat16),
            pltpu.SemaphoreType.DMA((2, NZ, NC)),
            pltpu.SemaphoreType.DMA((2, 2)),
            pltpu.SemaphoreType.DMA((2, NGLOBAL)),
            pltpu.SemaphoreType.DMA((Q_BLOCKS,)),
        ],
        compiler_params=pltpu.CompilerParams(vmem_limit_bytes=48 * 1024 * 1024),
        name="attend",
    )(meta, rand, q, full)


def return_kernel(a_ref, out_ref, zs, zr, ss, rs):
    xh, y, z, xl, c = coords()
    to_lo, to_sib = device(xh, y, z, 1 - xl, c), device(xh, y, z, xl, 1 - c)
    barrier = pltpu.get_barrier_semaphore()
    friends = [device(xh, y, (z + dz) % NZ, xl, c) for dz in range(1, NZ)] + [to_lo, to_sib]
    for friend in friends:
        pl.semaphore_signal(barrier, inc=1, device_id=friend, device_id_type=MESH)
    pl.semaphore_wait(barrier, len(friends))

    def place(half, side, plane):
        cols = pl.ds(pl.multiple_of((side * NZ + plane) * HEAD_DIM, HEAD_DIM), HEAD_DIM)
        return out_ref.at[pl.ds(pl.multiple_of(half * HALF, HALF), HALF), cols]

    def z_copy(k):
        t = (z + nearest(k) + NZ) % NZ
        return remote(a_ref.at[t], place(c, xl, z), zs.at[k], zr.at[z], device(xh, y, t, xl, c))

    def own():
        return pltpu.make_async_copy(a_ref.at[z], place(c, xl, z), zr.at[z])

    own().start()

    @pl.loop(1, NZ)
    def _(k):
        z_copy(k).start()

    def copy(cls, k, half, side, p, target):
        ref = place(half, side, p)
        return remote(ref, ref, ss.at[cls, k], rs.at[cls, k], target)

    @pl.loop(0, NZ + 1)
    def _(step):
        @pl.when(step > 0)
        def _():
            k = step - 1
            p = (z + nearest(k) + NZ) % NZ
            copy(0, k, c, 1 - xl, p, to_lo).wait_recv()
            copy(2, k, c, 1 - xl, p, to_sib).start()

        @pl.when(step < NZ)
        def _():
            p = (z + nearest(step) + NZ) % NZ
            remote(place(c, xl, p), place(c, xl, p), zs.at[0], zr.at[p], to_lo).wait_recv()
            copy(0, step, c, xl, p, to_lo).start()
            copy(1, step, c, xl, p, to_sib).start()

    @pl.loop(0, NZ)
    def _(k):
        p = (z + nearest(k) + NZ) % NZ

        @pl.when(k > 0)
        def _():
            z_copy(k).wait_send()

        copy(0, k, c, xl, p, to_lo).wait_send()
        copy(1, k, c, xl, p, to_sib).wait_send()
        copy(2, k, c, 1 - xl, p, to_sib).wait_send()
        copy(1, k, 1 - c, xl, p, to_sib).wait_recv()
        copy(2, k, 1 - c, 1 - xl, p, to_sib).wait_recv()


def return_call(attended):
    anyspace = pl.BlockSpec(memory_space=pl.ANY)
    return pl.pallas_call(
        return_kernel,
        out_shape=jax.ShapeDtypeStruct((ROWS, NXL * NZ * HEAD_DIM), jnp.bfloat16),
        in_specs=[anyspace],
        out_specs=anyspace,
        scratch_shapes=[
            pltpu.SemaphoreType.DMA((NZ,)),
            pltpu.SemaphoreType.DMA((NZ,)),
            pltpu.SemaphoreType.DMA((3, NZ)),
            pltpu.SemaphoreType.DMA((3, NZ)),
        ],
        compiler_params=pltpu.CompilerParams(collective_id=2, has_side_effects=True),
        name="return_attended",
    )(attended)


def address(block):
    shard, offset = block // SHARD_BLOCKS, block % SHARD_BLOCKS
    line, plane = shard // NZ, shard % NZ
    return ((line * NC + offset // HALF_BLOCKS) * NZ + plane) * HALF_BLOCKS + offset % HALF_BLOCKS


def body(queries, keys_values, global_ids, rand_ids, out_weight):
    xh, y, z, xl, c = coords()
    line = xh * NY + y
    total = LINES * LINE_BLOCKS
    lists = rand_ids.reshape(LINES, NZ, NC, HALF_BLOCKS * NRANDOM)
    mine = lax.dynamic_slice(lists, (line, 0, c, 0), (1, NZ, 1, HALF_BLOCKS * NRANDOM)).reshape(-1)
    rand = address(mine)
    edges = jnp.stack([line * LINE_BLOCKS - 1, line * LINE_BLOCKS + LINE_BLOCKS])
    blocks = jnp.concatenate([jnp.clip(edges, 0, total - 1), global_ids])
    meta = jnp.concatenate([jnp.stack([line, c]), address(blocks)])

    full, q = gather_call(queries, keys_values)
    full = full.reshape(2, total, BLOCK, HEAD_DIM)
    attended = attend_call(meta, rand, q.reshape(Q_BLOCKS, BLOCK, HEAD_DIM), full)
    everything = return_call(attended.reshape(NZ, HALF, HEAD_DIM))
    summed = jnp.dot(everything, out_weight, preferred_element_type=jnp.float32)
    return summed.astype(jnp.bfloat16)


def solution(mesh):
    in_specs = (P("seq", "head"), P(None, "seq", "head"), P(), P(), P(None, "head"))
    return jax.shard_map(body, mesh=mesh, in_specs=in_specs, out_specs=P("seq", "head"), check_vma=False)
```

```python
import math

import jax
import jax.numpy as jnp
from jax import lax
from jax.experimental import pallas as pl
from jax.experimental.pallas import tpu as pltpu
from jax.sharding import PartitionSpec as P

HEAD_DIM = 128
BLOCK = 64
NGLOBAL = 2
NRANDOM = 3
MESH = pl.DeviceIdType.MESH

NXH, NY, NZ, NXL, NC = 2, 4, 8, 2, 2
LINES = NXH * NY
SHARD_BLOCKS = 24
ROWS = SHARD_BLOCKS * BLOCK
HALF_BLOCKS = SHARD_BLOCKS // NC
HALF = HALF_BLOCKS * BLOCK
LINE_BLOCKS = NZ * SHARD_BLOCKS
Q_BLOCKS = NZ * HALF_BLOCKS


def coords():
    seq = lax.axis_index("seq")
    head = lax.axis_index("head")
    return seq // (NY * NZ), (seq // NZ) % NY, seq % NZ, head // NC, head % NC


def device(xh, y, z, xl, c):
    return ((xh * NY + y) * NZ + z, xl * NC + c)


def remote(src, dst, send_sem, recv_sem, target):
    return pltpu.make_async_remote_copy(
        src_ref=src, dst_ref=dst, send_sem=send_sem, recv_sem=recv_sem,
        device_id=target, device_id_type=MESH,
    )


def nearest(k):
    return (k % 2) * ((k + 1) // 2) - (1 - k % 2) * (k // 2)


X0, U1, D1, U2, D2, FU, FD, F2, G2 = range(9)
NCLASS = 9
ITEMS = 2 * NZ
SCORES_FROM = NZ + 3
SCALE = math.log2(math.e) / HEAD_DIM**0.5


def address(block):
    shard, offset = block // SHARD_BLOCKS, block % SHARD_BLOCKS
    line, plane = shard // NZ, shard % NZ
    return ((line * NC + offset // HALF_BLOCKS) * NZ + plane) * HALF_BLOCKS + offset % HALF_BLOCKS


def attention_kernel(table, q_ref, kv_ref, out_ref, kbuf, vbuf, qbuf, pbuf, obuf, zs, zr, cs, cr, bs, br, rzs, rzr, ras, rar):
    xh, y, z, xl, c = coords()
    line = xh * NY + y
    up, down, opp = (y + 1) % NY, (y + NY - 1) % NY, (y + 2) % NY
    ox = 1 - xh
    to_x, to_up, to_down = device(ox, y, z, xl, c), device(xh, up, z, xl, c), device(xh, down, z, xl, c)
    to_sib, to_lo = device(xh, y, z, xl, 1 - c), device(xh, y, z, 1 - xl, c)
    bufs = (kbuf, vbuf)

    barrier = pltpu.get_barrier_semaphore()
    friends = [
        device(xh, y, (z + dz) % NZ, xl, (c + dc) % NC)
        for dz in range(NZ) for dc in range(NC) if dz or dc
    ] + [to_x, to_up, to_down, to_lo]
    for friend in friends:
        pl.semaphore_signal(barrier, inc=1, device_id=friend, device_id_type=MESH)
    pl.semaphore_wait(barrier, len(friends))

    def piece(kv, ln, half, p):
        return bufs[kv].at[pl.ds(((ln * NC + half) * NZ + p) * HALF_BLOCKS, HALF_BLOCKS)]

    def near_plane(k):
        return (z + nearest(k) + NZ) % NZ

    def z_parts(t, kind, half):
        cols = pl.ds(pl.multiple_of((t - 4 * c) * HEAD_DIM, HEAD_DIM), HEAD_DIM)
        rows = pl.ds(half * HALF_BLOCKS, HALF_BLOCKS)
        if kind == 2:
            return q_ref.at[rows, :, cols], qbuf.at[pl.ds(z * HALF_BLOCKS, HALF_BLOCKS)]
        return kv_ref.at[kind, rows, :, cols], piece(kind, line, half, z)

    def z_each(k, kind, remote_fn, local_fn):
        t = near_plane(k)

        @pl.when(t // 4 == c)
        def _():
            for half in range(NC):
                src, dst = z_parts(t, kind, half)
                mine = jnp.logical_and(t == z, c == half)
                if local_fn is not None:
                    @pl.when(mine)
                    def _():
                        local_fn(pltpu.make_async_copy(src, dst, zr.at[kind, z]))

                @pl.when(jnp.logical_not(mine))
                def _():
                    remote_fn(remote(src, dst, zs.at[kind, half, k], zr.at[kind, z], device(xh, y, t, xl, half)))

    for kind in (0, 2, 1):
        @pl.loop(0, NZ)
        def _(k):
            z_each(k, kind, lambda d: d.start(), lambda d: d.start())

    H = HALF_BLOCKS // 2

    def at(xx, yy):
        return xx * NY + yy

    def copy(cls, e, p, kv, ln, target, rows=None):
        ref = piece(kv, ln, c, p)
        if rows is not None:
            ref = ref.at[pl.ds(rows * H, H)]
        return remote(ref, ref, cs.at[cls, e], cr.at[cls, e], target)

    def sib(e, p, kv, ln, half):
        ref = piece(kv, ln, half, p)
        return remote(ref, ref, bs.at[e, ln], br.at[e, ln], to_sib)

    shared = {
        U1: (at(xh, y), to_up, None, at(xh, down)), D1: (at(xh, y), to_down, None, at(xh, up)),
        X0: (at(xh, y), to_x, None, at(ox, y)),
        FU: (at(xh, down), to_up, 0, at(xh, opp)), FD: (at(xh, up), to_down, 1, at(xh, opp)),
    }
    x_first = dict(shared)
    x_first.update({
        U2: (at(ox, y), to_up, None, at(ox, down)), D2: (at(ox, y), to_down, None, at(ox, up)),
        F2: (at(ox, down), to_up, 0, at(ox, opp)), G2: (at(ox, up), to_down, 1, at(ox, opp)),
    })
    y_first = dict(shared)
    y_first.update({
        U2: (at(xh, down), to_x, None, at(ox, down)), D2: (at(xh, up), to_x, None, at(ox, up)),
        F2: (at(xh, opp), to_x, None, at(ox, opp)),
    })

    def is_x_first(kv, k):
        even = k % 2 == 0
        return even if kv == 0 else jnp.logical_or(even, k == NZ - 1)

    def modes(kv, k, body):
        first = is_x_first(kv, k)

        @pl.when(first)
        def _():
            body(x_first, True)

        @pl.when(jnp.logical_not(first))
        def _():
            body(y_first, False)

    def stages(kv, k, p, classes, xf, stage):
        e = kv * NZ + k

        def send(cls):
            ln, target, rows, _ = classes[cls]
            copy(cls, e, p, kv, ln, target, rows).start()

        def wait(cls):
            _, target, rows, ln = classes[cls]
            copy(cls, e, p, kv, ln, target, rows).wait_recv()

        def share(ln):
            sib(e, p, kv, ln, c).start()

        if stage == 1:
            ref = piece(kv, line, c, p)
            remote(ref, ref, zs.at[kv, 0, 0], zr.at[kv, p], to_x).wait_recv()
            for cls in (X0, U1, D1):
                send(cls)
            share(line)
        elif stage == 2 and xf:
            wait(X0)
            send(U2)
            send(D2)
            wait(U1)
            send(FU)
            wait(D1)
            send(FD)
            for ln in (at(ox, y), at(xh, down), at(xh, up)):
                share(ln)
        elif stage == 2:
            wait(U1)
            send(U2)
            send(FU)
            wait(D1)
            send(D2)
            send(FD)
            for ln in (at(xh, down), at(xh, up)):
                share(ln)
        elif stage == 3 and xf:
            wait(U2)
            send(F2)
            wait(D2)
            send(G2)
            wait(FU)
            wait(FD)
            for ln in (at(ox, down), at(ox, up), at(xh, opp)):
                share(ln)
        elif stage == 3:
            wait(FU)
            wait(FD)
            send(F2)
            wait(X0)
            for ln in (at(xh, opp), at(ox, y)):
                share(ln)
        elif xf:
            wait(F2)
            wait(G2)
            share(at(ox, opp))
        else:
            for cls, yy in ((U2, down), (D2, up), (F2, opp)):
                wait(cls)
                share(at(ox, yy))

    def sib_received(kv):
        @pl.loop(0, NZ)
        def _(k):
            p = near_plane(k)

            @pl.loop(0, LINES)
            def _(ln):
                sib(kv * NZ + k, p, kv, ln, 1 - c).wait_recv()

    column = lax.broadcasted_iota(jnp.int32, (1, 512), 1)
    globals_at = Q_BLOCKS * NRANDOM

    def listed(buf, n, block):
        last_block = LINES * LINE_BLOCKS - 1
        spots = [
            address(jnp.maximum(block - 1, 0)), address(block), address(jnp.minimum(block + 1, last_block)),
        ] + [table[n * NRANDOM + r] for r in range(NRANDOM)] + [table[globals_at + g] for g in range(NGLOBAL)]
        return jnp.concatenate([buf[s] for s in spots], axis=0)

    def doc_block(plane, o):
        return line * LINE_BLOCKS + plane * SHARD_BLOCKS + c * HALF_BLOCKS + o

    def weigh(plane, o):
        n, block = plane * HALF_BLOCKS + o, doc_block(plane, o)
        first = jnp.logical_and(block == 0, column < BLOCK)
        last = jnp.logical_and(
            block == LINES * LINE_BLOCKS - 1, jnp.logical_and(column >= 2 * BLOCK, column < 3 * BLOCK)
        )
        bias = jnp.where(jnp.logical_or(first, last), -jnp.inf, 0.0).astype(jnp.float32)
        scores = lax.dot_general(
            qbuf[n], listed(kbuf, n, block), (((1,), (1,)), ((), ())), preferred_element_type=jnp.float32
        )
        scores = scores * SCALE + bias
        powers = jnp.exp2(scores - jnp.max(scores, axis=1, keepdims=True))
        pbuf[n] = (powers * (1.0 / jnp.sum(powers, axis=1, keepdims=True))).astype(jnp.bfloat16)

    def mix(plane, o):
        n, block = plane * HALF_BLOCKS + o, doc_block(plane, o)
        mixed = jnp.dot(pbuf[n], listed(vbuf, n, block), preferred_element_type=jnp.float32)
        obuf[n] = mixed.astype(jnp.bfloat16)

    def blocks_of(plane, fn):
        @pl.loop(0, HALF_BLOCKS // 4)
        def _(m):
            for u in range(4):
                fn(plane, m * 4 + u)

    @pl.loop(0, ITEMS + 3)
    def _(step):
        for stage in (4, 3, 2, 1):
            e = step - (stage - 1)
            for kv in range(2):
                @pl.when(jnp.logical_and(e >= kv * NZ, e < (kv + 1) * NZ))
                def _():
                    k = e - kv * NZ
                    p = near_plane(k)
                    modes(kv, k, lambda classes, xf: stages(kv, k, p, classes, xf, stage))

        @pl.when(step == SCORES_FROM)
        def _():
            sib_received(0)

            @pl.loop(0, NZ)
            def _(p):
                ref = qbuf.at[pl.ds(p * HALF_BLOCKS, HALF_BLOCKS)]
                remote(ref, ref, zs.at[2, 0, 0], zr.at[2, p], to_x).wait_recv()

        @pl.when(step >= SCORES_FROM)
        def _():
            blocks_of(step - SCORES_FROM, weigh)

    sib_received(1)

    def place(half, side, plane):
        cols = pl.ds(pl.multiple_of((side * NZ + plane) * HEAD_DIM, HEAD_DIM), HEAD_DIM)
        return out_ref.at[pl.ds(half * HALF_BLOCKS, HALF_BLOCKS), :, cols]

    def rows_of(p):
        return obuf.at[pl.ds(p * HALF_BLOCKS, HALF_BLOCKS)]

    def home(k, p):
        return remote(rows_of(p), place(c, xl, z), rzs.at[k], rzr.at[z], device(xh, y, p, xl, c))

    def onward(cls, k, half, side, p, target):
        ref = place(half, side, p)
        return remote(ref, ref, ras.at[cls, k], rar.at[cls, k], target)

    @pl.loop(0, NZ + 4)
    def _(step):
        @pl.when(step < NZ)
        def _():
            p = near_plane(step)
            blocks_of(p, mix)

            @pl.when(step == 0)
            def _():
                pltpu.make_async_copy(rows_of(z), place(c, xl, z), rzr.at[z]).start()

            @pl.when(step > 0)
            def _():
                home(step, p).start()

        @pl.when(jnp.logical_and(step >= 2, step < NZ + 2))
        def _():
            k = step - 2
            p = near_plane(k)
            remote(place(c, xl, p), place(c, xl, p), rzs.at[0], rzr.at[p], to_lo).wait_recv()
            onward(0, k, c, xl, p, to_lo).start()
            onward(1, k, c, xl, p, to_sib).start()

        @pl.when(step >= 4)
        def _():
            k = step - 4
            p = near_plane(k)
            onward(0, k, c, 1 - xl, p, to_lo).wait_recv()
            onward(2, k, c, 1 - xl, p, to_sib).start()

    @pl.loop(0, NZ)
    def _(k):
        p = near_plane(k)

        @pl.when(k > 0)
        def _():
            home(k, p).wait_send()

        onward(0, k, c, xl, p, to_lo).wait_send()
        onward(1, k, c, xl, p, to_sib).wait_send()
        onward(2, k, c, 1 - xl, p, to_sib).wait_send()
        onward(1, k, 1 - c, xl, p, to_sib).wait_recv()
        onward(2, k, 1 - c, 1 - xl, p, to_sib).wait_recv()
        for kind in range(3):
            z_each(k, kind, lambda d: d.wait_send(), None)
        for kv in range(2):
            e = kv * NZ + k

            def sent(classes, xf):
                for cls, (ln, target, rows, _) in classes.items():
                    copy(cls, e, p, kv, ln, target, rows).wait_send()

            modes(kv, k, sent)

            @pl.loop(0, LINES)
            def _(ln):
                sib(e, p, kv, ln, c).wait_send()


def attention_call(table, queries, keys_values):
    anyspace = pl.BlockSpec(memory_space=pl.ANY)
    dma = pltpu.SemaphoreType.DMA
    key_blocks = LINES * LINE_BLOCKS
    return pl.pallas_call(
        attention_kernel,
        out_shape=jax.ShapeDtypeStruct((SHARD_BLOCKS, BLOCK, NXL * NZ * HEAD_DIM), jnp.bfloat16),
        in_specs=[pl.BlockSpec(memory_space=pltpu.SMEM), anyspace, anyspace],
        out_specs=anyspace,
        scratch_shapes=[
            pltpu.VMEM((key_blocks, BLOCK, HEAD_DIM), jnp.bfloat16),
            pltpu.VMEM((key_blocks, BLOCK, HEAD_DIM), jnp.bfloat16),
            pltpu.VMEM((Q_BLOCKS, BLOCK, HEAD_DIM), jnp.bfloat16),
            pltpu.VMEM((Q_BLOCKS, BLOCK, 512), jnp.bfloat16),
            pltpu.VMEM((Q_BLOCKS, BLOCK, HEAD_DIM), jnp.bfloat16),
            dma((3, NC, NZ)), dma((3, NZ)),
            dma((NCLASS, ITEMS)), dma((NCLASS, ITEMS)),
            dma((ITEMS, LINES)), dma((ITEMS, LINES)),
            dma((NZ,)), dma((NZ,)), dma((3, NZ)), dma((3, NZ)),
        ],
        compiler_params=pltpu.CompilerParams(
            collective_id=1, has_side_effects=True, vmem_limit_bytes=60 * 1024 * 1024
        ),
        name="block_attention",
    )(table, queries, keys_values)


def body(queries, keys_values, global_ids, rand_ids, out_weight):
    xh, y, z, xl, c = coords()
    width = queries.shape[1]
    lists = rand_ids.reshape(LINES, NZ, NC, HALF_BLOCKS * NRANDOM)
    mine = lax.dynamic_slice(lists, (xh * NY + y, 0, c, 0), (1, NZ, 1, HALF_BLOCKS * NRANDOM)).reshape(-1)
    table = address(jnp.concatenate([mine, global_ids]))
    attended = attention_call(
        table,
        queries.reshape(SHARD_BLOCKS, BLOCK, width),
        keys_values.reshape(2, SHARD_BLOCKS, BLOCK, width),
    )
    summed = jnp.dot(attended.reshape(ROWS, -1), out_weight, preferred_element_type=jnp.float32)
    return summed.astype(jnp.bfloat16)


def solution(mesh):
    in_specs = (P("seq", "head"), P(None, "seq", "head"), P(), P(), P(None, "head"))
    return jax.shard_map(body, mesh=mesh, in_specs=in_specs, out_specs=P("seq", "head"), check_vma=False)
```

```python
import math

import jax
import jax.numpy as jnp
from jax import lax
from jax.experimental import pallas as pl
from jax.experimental.pallas import tpu as pltpu
from jax.sharding import PartitionSpec as P

HEAD_DIM = 128
BLOCK = 64
NGLOBAL = 2
NRANDOM = 3
MESH = pl.DeviceIdType.MESH

NXH, NY, NZ, NXL, NC = 2, 4, 8, 2, 2
LINES = NXH * NY
SHARD_BLOCKS = 24
ROWS = SHARD_BLOCKS * BLOCK
HALF_BLOCKS = SHARD_BLOCKS // NC
HALF = HALF_BLOCKS * BLOCK
LINE_BLOCKS = NZ * SHARD_BLOCKS
Q_BLOCKS = NZ * HALF_BLOCKS


def coords():
    seq = lax.axis_index("seq")
    head = lax.axis_index("head")
    return seq // (NY * NZ), (seq // NZ) % NY, seq % NZ, head // NC, head % NC


def device(xh, y, z, xl, c):
    return ((xh * NY + y) * NZ + z, xl * NC + c)


def remote(src, dst, send_sem, recv_sem, target):
    return pltpu.make_async_remote_copy(
        src_ref=src, dst_ref=dst, send_sem=send_sem, recv_sem=recv_sem,
        device_id=target, device_id_type=MESH,
    )


def nearest(k):
    return (k % 2) * ((k + 1) // 2) - (1 - k % 2) * (k // 2)


X0, U1, D1, U2, D2, FU, FD, YU, YD, F2, G2, YO = range(12)
NCLASS = 12
FROM_X = (7, 6)
Z_LEAD = 2
ITEMS = 2 * NZ
DELAY = (0, 0, 2, 4, 6)
SCORES_FROM = NZ + DELAY[4]
SCALE = math.log2(math.e) / HEAD_DIM**0.5


def address(block):
    shard, offset = block // SHARD_BLOCKS, block % SHARD_BLOCKS
    line, plane = shard // NZ, shard % NZ
    return ((line * NC + offset // HALF_BLOCKS) * NZ + plane) * HALF_BLOCKS + offset % HALF_BLOCKS


def attention_kernel(table, q_ref, kv_ref, out_ref, kbuf, vbuf, qbuf, pbuf, obuf, zs, zr, cs, cr, bs, br, rzs, rzr, ras, rar):
    xh, y, z, xl, c = coords()
    line = xh * NY + y
    up, down, opp = (y + 1) % NY, (y + NY - 1) % NY, (y + 2) % NY
    ox = 1 - xh
    to_x, to_up, to_down = device(ox, y, z, xl, c), device(xh, up, z, xl, c), device(xh, down, z, xl, c)
    to_sib, to_lo = device(xh, y, z, xl, 1 - c), device(xh, y, z, 1 - xl, c)
    bufs = (kbuf, vbuf)

    barrier = pltpu.get_barrier_semaphore()
    friends = [
        device(xh, y, (z + dz) % NZ, xl, (c + dc) % NC)
        for dz in range(NZ) for dc in range(NC) if dz or dc
    ] + [to_x, to_up, to_down, to_lo]
    for friend in friends:
        pl.semaphore_signal(barrier, inc=1, device_id=friend, device_id_type=MESH)
    pl.semaphore_wait(barrier, len(friends))

    def piece(kv, ln, half, p):
        return bufs[kv].at[pl.ds(((ln * NC + half) * NZ + p) * HALF_BLOCKS, HALF_BLOCKS)]

    def near_plane(k):
        return (z + nearest(k) + NZ) % NZ

    def z_parts(t, kind, half):
        cols = pl.ds(pl.multiple_of((t - 4 * c) * HEAD_DIM, HEAD_DIM), HEAD_DIM)
        rows = pl.ds(half * HALF_BLOCKS, HALF_BLOCKS)
        if kind == 2:
            return q_ref.at[rows, :, cols], qbuf.at[pl.ds(z * HALF_BLOCKS, HALF_BLOCKS)]
        return kv_ref.at[kind, rows, :, cols], piece(kind, line, half, z)

    def z_each(k, kind, remote_fn, local_fn):
        t = near_plane(k)

        @pl.when(t // 4 == c)
        def _():
            for half in range(NC):
                src, dst = z_parts(t, kind, half)
                mine = jnp.logical_and(t == z, c == half)
                if local_fn is not None:
                    @pl.when(mine)
                    def _():
                        local_fn(pltpu.make_async_copy(src, dst, zr.at[kind, z]))

                @pl.when(jnp.logical_not(mine))
                def _():
                    remote_fn(remote(src, dst, zs.at[kind, half, k], zr.at[kind, z], device(xh, y, t, xl, half)))

    def z_start(k, kind):
        z_each(k, kind, lambda d: d.start(), lambda d: d.start())

    @pl.loop(0, Z_LEAD)
    def _(k):
        z_start(k, 0)

    H = HALF_BLOCKS // 2

    def at(xx, yy):
        return xx * NY + yy

    def routes(kv):
        m = FROM_X[kv]
        h = (m + 1) // 2
        rest = (m, HALF_BLOCKS - m)
        return {
            X0: (line, to_x, (0, HALF_BLOCKS), at(ox, y)),
            U1: (line, to_up, (0, HALF_BLOCKS), at(xh, down)),
            D1: (line, to_down, (0, HALF_BLOCKS), at(xh, up)),
            U2: (at(ox, y), to_up, (0, m), at(ox, down)),
            D2: (at(ox, y), to_down, (0, m), at(ox, up)),
            FU: (at(xh, down), to_up, (0, H), at(xh, opp)),
            FD: (at(xh, up), to_down, (H, H), at(xh, opp)),
            YU: (at(xh, down), to_x, rest, at(ox, down)),
            YD: (at(xh, up), to_x, rest, at(ox, up)),
            F2: (at(ox, down), to_up, (0, h), at(ox, opp)),
            G2: (at(ox, up), to_down, (h, m - h), at(ox, opp)),
            YO: (at(xh, opp), to_x, rest, at(ox, opp)),
        }

    def copy(cls, e, p, kv, ln, target, span):
        ref = piece(kv, ln, c, p).at[pl.ds(*span)]
        return remote(ref, ref, cs.at[cls, e], cr.at[cls, e], target)

    def sib(e, p, kv, ln, half):
        ref = piece(kv, ln, half, p)
        return remote(ref, ref, bs.at[e, ln], br.at[e, ln], to_sib)

    def stages(kv, k, p, stage):
        e = kv * NZ + k
        classes = routes(kv)

        def send(*names):
            for cls in names:
                ln, target, span, _ = classes[cls]
                copy(cls, e, p, kv, ln, target, span).start()

        def wait(*names):
            for cls in names:
                _, target, span, ln = classes[cls]
                copy(cls, e, p, kv, ln, target, span).wait_recv()

        def share(*lines):
            for ln in lines:
                sib(e, p, kv, ln, c).start()

        if stage == 1:
            ref = piece(kv, line, c, p)
            remote(ref, ref, zs.at[kv, 0, 0], zr.at[kv, p], to_x).wait_recv()
            send(X0, U1, D1)
            share(line)
        elif stage == 2:
            wait(X0)
            send(U2, D2)
            wait(U1)
            send(YU, FU)
            wait(D1)
            send(YD, FD)
            share(at(ox, y), at(xh, down), at(xh, up))
        elif stage == 3:
            wait(U2)
            send(F2)
            wait(D2)
            send(G2)
            wait(FU, FD)
            send(YO)
            share(at(xh, opp))
        else:
            wait(YU, YD)
            share(at(ox, down), at(ox, up))
            wait(F2, G2, YO)
            share(at(ox, opp))

    def sib_received(kv):
        @pl.loop(0, NZ)
        def _(k):
            p = near_plane(k)

            @pl.loop(0, LINES)
            def _(ln):
                sib(kv * NZ + k, p, kv, ln, 1 - c).wait_recv()

    column = lax.broadcasted_iota(jnp.int32, (1, 512), 1)
    globals_at = Q_BLOCKS * NRANDOM

    def listed(buf, n, block):
        last_block = LINES * LINE_BLOCKS - 1
        spots = [
            address(jnp.maximum(block - 1, 0)), address(block), address(jnp.minimum(block + 1, last_block)),
        ] + [table[n * NRANDOM + r] for r in range(NRANDOM)] + [table[globals_at + g] for g in range(NGLOBAL)]
        return jnp.concatenate([buf[s] for s in spots], axis=0)

    def doc_block(plane, o):
        return line * LINE_BLOCKS + plane * SHARD_BLOCKS + c * HALF_BLOCKS + o

    def weigh(plane, o):
        n, block = plane * HALF_BLOCKS + o, doc_block(plane, o)
        first = jnp.logical_and(block == 0, column < BLOCK)
        last = jnp.logical_and(
            block == LINES * LINE_BLOCKS - 1, jnp.logical_and(column >= 2 * BLOCK, column < 3 * BLOCK)
        )
        bias = jnp.where(jnp.logical_or(first, last), -jnp.inf, 0.0).astype(jnp.float32)
        scores = lax.dot_general(
            qbuf[n], listed(kbuf, n, block), (((1,), (1,)), ((), ())), preferred_element_type=jnp.float32
        )
        scores = scores * SCALE + bias
        powers = jnp.exp2(scores - jnp.max(scores, axis=1, keepdims=True))
        pbuf[n] = (powers * (1.0 / jnp.sum(powers, axis=1, keepdims=True))).astype(jnp.bfloat16)

    def mix(plane, o):
        n, block = plane * HALF_BLOCKS + o, doc_block(plane, o)
        mixed = jnp.dot(pbuf[n], listed(vbuf, n, block), preferred_element_type=jnp.float32)
        obuf[n] = mixed.astype(jnp.bfloat16)

    def blocks_of(plane, fn):
        @pl.loop(0, HALF_BLOCKS // 4)
        def _(m):
            for u in range(4):
                fn(plane, m * 4 + u)

    @pl.loop(0, ITEMS + DELAY[4])
    def _(step):
        for kind, lag in ((0, -Z_LEAD), (1, 5), (2, 6)):
            @pl.when(jnp.logical_and(step >= max(lag, 0), step < NZ + lag))
            def _():
                z_start(step - lag, kind)

        for stage in (4, 3, 2, 1):
            e = step - DELAY[stage]
            for kv in range(2):
                @pl.when(jnp.logical_and(e >= kv * NZ, e < (kv + 1) * NZ))
                def _():
                    k = e - kv * NZ
                    p = near_plane(k)
                    stages(kv, k, p, stage)

        @pl.when(step == SCORES_FROM)
        def _():
            sib_received(0)

            @pl.loop(0, NZ)
            def _(p):
                ref = qbuf.at[pl.ds(p * HALF_BLOCKS, HALF_BLOCKS)]
                remote(ref, ref, zs.at[2, 0, 0], zr.at[2, p], to_x).wait_recv()

        @pl.when(step >= SCORES_FROM)
        def _():
            blocks_of(step - SCORES_FROM, weigh)

    sib_received(1)

    def place(half, side, plane):
        cols = pl.ds(pl.multiple_of((side * NZ + plane) * HEAD_DIM, HEAD_DIM), HEAD_DIM)
        return out_ref.at[pl.ds(half * HALF_BLOCKS, HALF_BLOCKS), :, cols]

    def rows_of(p):
        return obuf.at[pl.ds(p * HALF_BLOCKS, HALF_BLOCKS)]

    def home(k, p):
        return remote(rows_of(p), place(c, xl, z), rzs.at[k], rzr.at[z], device(xh, y, p, xl, c))

    def onward(cls, k, half, side, p, target):
        ref = place(half, side, p)
        return remote(ref, ref, ras.at[cls, k], rar.at[cls, k], target)

    @pl.loop(0, NZ + 4)
    def _(step):
        @pl.when(step < NZ)
        def _():
            p = near_plane(step)
            blocks_of(p, mix)

            @pl.when(step == 0)
            def _():
                pltpu.make_async_copy(rows_of(z), place(c, xl, z), rzr.at[z]).start()

            @pl.when(step > 0)
            def _():
                home(step, p).start()

        @pl.when(jnp.logical_and(step >= 2, step < NZ + 2))
        def _():
            k = step - 2
            p = near_plane(k)
            remote(place(c, xl, p), place(c, xl, p), rzs.at[0], rzr.at[p], to_lo).wait_recv()
            onward(0, k, c, xl, p, to_lo).start()
            onward(1, k, c, xl, p, to_sib).start()

        @pl.when(step >= 4)
        def _():
            k = step - 4
            p = near_plane(k)
            onward(0, k, c, 1 - xl, p, to_lo).wait_recv()
            onward(2, k, c, 1 - xl, p, to_sib).start()

    @pl.loop(0, NZ)
    def _(k):
        p = near_plane(k)

        @pl.when(k > 0)
        def _():
            home(k, p).wait_send()

        onward(0, k, c, xl, p, to_lo).wait_send()
        onward(1, k, c, xl, p, to_sib).wait_send()
        onward(2, k, c, 1 - xl, p, to_sib).wait_send()
        onward(1, k, 1 - c, xl, p, to_sib).wait_recv()
        onward(2, k, 1 - c, 1 - xl, p, to_sib).wait_recv()
        for kind in range(3):
            z_each(k, kind, lambda d: d.wait_send(), None)
        for kv in range(2):
            e = kv * NZ + k

            for cls, (ln, target, span, _) in routes(kv).items():
                copy(cls, e, p, kv, ln, target, span).wait_send()

            @pl.loop(0, LINES)
            def _(ln):
                sib(e, p, kv, ln, c).wait_send()


def attention_call(table, queries, keys_values):
    anyspace = pl.BlockSpec(memory_space=pl.ANY)
    dma = pltpu.SemaphoreType.DMA
    key_blocks = LINES * LINE_BLOCKS
    return pl.pallas_call(
        attention_kernel,
        out_shape=jax.ShapeDtypeStruct((SHARD_BLOCKS, BLOCK, NXL * NZ * HEAD_DIM), jnp.bfloat16),
        in_specs=[pl.BlockSpec(memory_space=pltpu.SMEM), anyspace, anyspace],
        out_specs=anyspace,
        scratch_shapes=[
            pltpu.VMEM((key_blocks, BLOCK, HEAD_DIM), jnp.bfloat16),
            pltpu.VMEM((key_blocks, BLOCK, HEAD_DIM), jnp.bfloat16),
            pltpu.VMEM((Q_BLOCKS, BLOCK, HEAD_DIM), jnp.bfloat16),
            pltpu.VMEM((Q_BLOCKS, BLOCK, 512), jnp.bfloat16),
            pltpu.VMEM((Q_BLOCKS, BLOCK, HEAD_DIM), jnp.bfloat16),
            dma((3, NC, NZ)), dma((3, NZ)),
            dma((NCLASS, ITEMS)), dma((NCLASS, ITEMS)),
            dma((ITEMS, LINES)), dma((ITEMS, LINES)),
            dma((NZ,)), dma((NZ,)), dma((3, NZ)), dma((3, NZ)),
        ],
        compiler_params=pltpu.CompilerParams(
            collective_id=1, has_side_effects=True, vmem_limit_bytes=60 * 1024 * 1024
        ),
        name="block_attention",
    )(table, queries, keys_values)


def body(queries, keys_values, global_ids, rand_ids, out_weight):
    xh, y, z, xl, c = coords()
    width = queries.shape[1]
    lists = rand_ids.reshape(LINES, NZ, NC, HALF_BLOCKS * NRANDOM)
    mine = lax.dynamic_slice(lists, (xh * NY + y, 0, c, 0), (1, NZ, 1, HALF_BLOCKS * NRANDOM)).reshape(-1)
    table = address(jnp.concatenate([mine, global_ids]))
    attended = attention_call(
        table,
        queries.reshape(SHARD_BLOCKS, BLOCK, width),
        keys_values.reshape(2, SHARD_BLOCKS, BLOCK, width),
    )
    summed = jnp.dot(attended.reshape(ROWS, -1), out_weight, preferred_element_type=jnp.float32)
    return summed.astype(jnp.bfloat16)


def solution(mesh):
    in_specs = (P("seq", "head"), P(None, "seq", "head"), P(), P(), P(None, "head"))
    return jax.shard_map(body, mesh=mesh, in_specs=in_specs, out_specs=P("seq", "head"), check_vma=False)
```

```python
import math

import jax
import jax.numpy as jnp
from jax import lax
from jax.experimental import pallas as pl
from jax.experimental.pallas import tpu as pltpu
from jax.sharding import PartitionSpec as P

HEAD_DIM = 128
BLOCK = 64
NGLOBAL = 2
NRANDOM = 3
MESH = pl.DeviceIdType.MESH

NXH, NY, NZ, NXL, NC = 2, 4, 8, 2, 2
LINES = NXH * NY
SHARD_BLOCKS = 24
ROWS = SHARD_BLOCKS * BLOCK
HALF_BLOCKS = SHARD_BLOCKS // NC
HALF = HALF_BLOCKS * BLOCK
LINE_BLOCKS = NZ * SHARD_BLOCKS
Q_BLOCKS = NZ * HALF_BLOCKS


def coords():
    seq = lax.axis_index("seq")
    head = lax.axis_index("head")
    return seq // (NY * NZ), (seq // NZ) % NY, seq % NZ, head // NC, head % NC


def device(xh, y, z, xl, c):
    return ((xh * NY + y) * NZ + z, xl * NC + c)


def remote(src, dst, send_sem, recv_sem, target):
    return pltpu.make_async_remote_copy(
        src_ref=src, dst_ref=dst, send_sem=send_sem, recv_sem=recv_sem,
        device_id=target, device_id_type=MESH,
    )


def nearest(k):
    return (k % 2) * ((k + 1) // 2) - (1 - k % 2) * (k // 2)


X0, U1, D1, U2, D2, FU, FD, YU, YD, F2, G2, YO = range(12)
NCLASS = 12
FROM_X = (7, 6)
Z_LEAD = 2
ITEMS = 2 * NZ
CHUNK = 4
PARTS = NZ * HALF_BLOCKS // CHUNK
LAG = 3
WEIGHT_AT = 512
DELAY = (0, 0, 2, 4, 6)
SCORES_FROM = NZ + DELAY[4]
SCALE = math.log2(math.e) / HEAD_DIM**0.5


def address(block):
    shard, offset = block // SHARD_BLOCKS, block % SHARD_BLOCKS
    line, plane = shard // NZ, shard % NZ
    return ((line * NC + offset // HALF_BLOCKS) * NZ + plane) * HALF_BLOCKS + offset % HALF_BLOCKS


def attention_kernel(
    table, q_ref, kv_ref, w_ref, out_ref, kbuf, vbuf, qbuf, pbuf, obuf,
    zs, zr, cs, cr, bs, br, rzs, rzr, ras, rar, ws, os, ready,
):
    xh, y, z, xl, c = coords()
    line = xh * NY + y
    up, down, opp = (y + 1) % NY, (y + NY - 1) % NY, (y + 2) % NY
    ox = 1 - xh
    to_x, to_up, to_down = device(ox, y, z, xl, c), device(xh, up, z, xl, c), device(xh, down, z, xl, c)
    to_sib, to_lo = device(xh, y, z, xl, 1 - c), device(xh, y, z, 1 - xl, c)
    bufs = (kbuf, vbuf)

    barrier = pltpu.get_barrier_semaphore()
    friends = [
        device(xh, y, (z + dz) % NZ, xl, (c + dc) % NC)
        for dz in range(NZ) for dc in range(NC) if dz or dc
    ] + [to_x, to_up, to_down, to_lo]
    for friend in friends:
        pl.semaphore_signal(barrier, inc=1, device_id=friend, device_id_type=MESH)
    pl.semaphore_wait(barrier, len(friends))

    def piece(kv, ln, half, p):
        return bufs[kv].at[pl.ds(((ln * NC + half) * NZ + p) * HALF_BLOCKS, HALF_BLOCKS)]

    def near_plane(k):
        return (z + nearest(k) + NZ) % NZ

    def z_parts(t, kind, half):
        cols = pl.ds(pl.multiple_of((t - 4 * c) * HEAD_DIM, HEAD_DIM), HEAD_DIM)
        rows = pl.ds(half * HALF_BLOCKS, HALF_BLOCKS)
        if kind == 2:
            return q_ref.at[rows, :, cols], qbuf.at[pl.ds(z * HALF_BLOCKS, HALF_BLOCKS)]
        return kv_ref.at[kind, rows, :, cols], piece(kind, line, half, z)

    def z_each(k, kind, remote_fn, local_fn):
        t = near_plane(k)

        @pl.when(t // 4 == c)
        def _():
            for half in range(NC):
                src, dst = z_parts(t, kind, half)
                mine = jnp.logical_and(t == z, c == half)
                if local_fn is not None:
                    @pl.when(mine)
                    def _():
                        local_fn(pltpu.make_async_copy(src, dst, zr.at[kind, z]))

                @pl.when(jnp.logical_not(mine))
                def _():
                    remote_fn(remote(src, dst, zs.at[kind, half, k], zr.at[kind, z], device(xh, y, t, xl, half)))

    def z_start(k, kind):
        z_each(k, kind, lambda d: d.start(), lambda d: d.start())

    @pl.loop(0, Z_LEAD)
    def _(k):
        z_start(k, 0)

    H = HALF_BLOCKS // 2

    def at(xx, yy):
        return xx * NY + yy

    def routes(kv):
        m = FROM_X[kv]
        h = (m + 1) // 2
        rest = (m, HALF_BLOCKS - m)
        return {
            X0: (line, to_x, (0, HALF_BLOCKS), at(ox, y)),
            U1: (line, to_up, (0, HALF_BLOCKS), at(xh, down)),
            D1: (line, to_down, (0, HALF_BLOCKS), at(xh, up)),
            U2: (at(ox, y), to_up, (0, m), at(ox, down)),
            D2: (at(ox, y), to_down, (0, m), at(ox, up)),
            FU: (at(xh, down), to_up, (0, H), at(xh, opp)),
            FD: (at(xh, up), to_down, (H, H), at(xh, opp)),
            YU: (at(xh, down), to_x, rest, at(ox, down)),
            YD: (at(xh, up), to_x, rest, at(ox, up)),
            F2: (at(ox, down), to_up, (0, h), at(ox, opp)),
            G2: (at(ox, up), to_down, (h, m - h), at(ox, opp)),
            YO: (at(xh, opp), to_x, rest, at(ox, opp)),
        }

    def copy(cls, e, p, kv, ln, target, span):
        ref = piece(kv, ln, c, p).at[pl.ds(*span)]
        return remote(ref, ref, cs.at[cls, e], cr.at[cls, e], target)

    def sib(e, p, kv, ln, half):
        ref = piece(kv, ln, half, p)
        return remote(ref, ref, bs.at[e, ln], br.at[e, ln], to_sib)

    def stages(kv, k, p, stage):
        e = kv * NZ + k
        classes = routes(kv)

        def send(*names):
            for cls in names:
                ln, target, span, _ = classes[cls]
                copy(cls, e, p, kv, ln, target, span).start()

        def wait(*names):
            for cls in names:
                _, target, span, ln = classes[cls]
                copy(cls, e, p, kv, ln, target, span).wait_recv()

        def share(*lines):
            for ln in lines:
                sib(e, p, kv, ln, c).start()

        if stage == 1:
            ref = piece(kv, line, c, p)
            remote(ref, ref, zs.at[kv, 0, 0], zr.at[kv, p], to_x).wait_recv()
            send(X0, U1, D1)
            share(line)
        elif stage == 2:
            wait(X0)
            send(U2, D2)
            wait(U1)
            send(YU, FU)
            wait(D1)
            send(YD, FD)
            share(at(ox, y), at(xh, down), at(xh, up))
        elif stage == 3:
            wait(U2)
            send(F2)
            wait(D2)
            send(G2)
            wait(FU, FD)
            send(YO)
            share(at(xh, opp))
        else:
            wait(YU, YD)
            share(at(ox, down), at(ox, up))
            wait(F2, G2, YO)
            share(at(ox, opp))

    def sib_received(kv):
        @pl.loop(0, NZ)
        def _(k):
            p = near_plane(k)

            @pl.loop(0, LINES)
            def _(ln):
                sib(kv * NZ + k, p, kv, ln, 1 - c).wait_recv()

    column = lax.broadcasted_iota(jnp.int32, (1, 512), 1)
    globals_at = Q_BLOCKS * NRANDOM

    def listed(buf, n, block):
        last_block = LINES * LINE_BLOCKS - 1
        spots = [
            address(jnp.maximum(block - 1, 0)), address(block), address(jnp.minimum(block + 1, last_block)),
        ] + [table[n * NRANDOM + r] for r in range(NRANDOM)] + [table[globals_at + g] for g in range(NGLOBAL)]
        return jnp.concatenate([buf[s] for s in spots], axis=0)

    def doc_block(plane, o):
        return line * LINE_BLOCKS + plane * SHARD_BLOCKS + c * HALF_BLOCKS + o

    def weigh(plane, o):
        n, block = plane * HALF_BLOCKS + o, doc_block(plane, o)
        first = jnp.logical_and(block == 0, column < BLOCK)
        last = jnp.logical_and(
            block == LINES * LINE_BLOCKS - 1, jnp.logical_and(column >= 2 * BLOCK, column < 3 * BLOCK)
        )
        bias = jnp.where(jnp.logical_or(first, last), -jnp.inf, 0.0).astype(jnp.float32)
        scores = lax.dot_general(
            qbuf[n], listed(kbuf, n, block), (((1,), (1,)), ((), ())), preferred_element_type=jnp.float32
        )
        scores = scores * SCALE + bias
        powers = jnp.exp2(scores - jnp.max(scores, axis=1, keepdims=True))
        pbuf[n] = (powers * (1.0 / jnp.sum(powers, axis=1, keepdims=True))).astype(jnp.bfloat16)

    def mix(plane, o):
        n, block = plane * HALF_BLOCKS + o, doc_block(plane, o)
        mixed = jnp.dot(pbuf[n], listed(vbuf, n, block), preferred_element_type=jnp.float32)
        obuf[n] = mixed.astype(jnp.bfloat16)

    def weight_copy(g):
        cols = pl.ds(pl.multiple_of(g * HEAD_DIM, HEAD_DIM), HEAD_DIM)
        return pltpu.make_async_copy(w_ref.at[:, :, cols], kbuf.at[pl.ds(WEIGHT_AT + g * 32, 32)], ws.at[g])

    writers = [device(xh, y, (z + dz) % NZ, xl, c) for dz in range(1, NZ)] + [to_lo, to_sib]

    def sends_done(kv):
        @pl.loop(0, NZ)
        def _(k):
            p = near_plane(k)
            e = kv * NZ + k
            for cls, (ln, target, span, _) in routes(kv).items():
                copy(cls, e, p, kv, ln, target, span).wait_send()

            @pl.loop(0, LINES)
            def _(ln):
                sib(e, p, kv, ln, c).wait_send()

    def blocks_of(plane, fn):
        @pl.loop(0, HALF_BLOCKS // 4)
        def _(m):
            for u in range(4):
                fn(plane, m * 4 + u)

    @pl.loop(0, ITEMS + DELAY[4])
    def _(step):
        for kind, lag in ((0, -Z_LEAD), (1, 5), (2, 6)):
            @pl.when(jnp.logical_and(step >= max(lag, 0), step < NZ + lag))
            def _():
                z_start(step - lag, kind)

        for stage in (4, 3, 2, 1):
            e = step - DELAY[stage]
            for kv in range(2):
                @pl.when(jnp.logical_and(e >= kv * NZ, e < (kv + 1) * NZ))
                def _():
                    k = e - kv * NZ
                    p = near_plane(k)
                    stages(kv, k, p, stage)

        @pl.when(step == SCORES_FROM)
        def _():
            sib_received(0)

            @pl.loop(0, NZ)
            def _(p):
                ref = qbuf.at[pl.ds(p * HALF_BLOCKS, HALF_BLOCKS)]
                remote(ref, ref, zs.at[2, 0, 0], zr.at[2, p], to_x).wait_recv()

        @pl.when(jnp.logical_and(step >= SCORES_FROM, step < SCORES_FROM + NZ // 2))
        def _():
            for u in range(2):
                blocks_of(2 * (step - SCORES_FROM) + u, weigh)

        @pl.when(step == SCORES_FROM + NZ // 2)
        def _():
            sends_done(0)

            @pl.loop(0, NZ)
            def _(g):
                weight_copy(g).start()

            for writer in writers:
                pl.semaphore_signal(ready, inc=1, device_id=writer, device_id_type=MESH)

    sib_received(1)

    def place(half, side, plane, r):
        return kbuf.at[pl.ds((side * NZ + plane) * SHARD_BLOCKS + half * HALF_BLOCKS + r * CHUNK, CHUNK)]

    def rows_of(p, r):
        return obuf.at[pl.ds(p * HALF_BLOCKS + r * CHUNK, CHUNK)]

    def home(r, k, p):
        return remote(rows_of(p, r), place(c, xl, z, r), rzs.at[r, k], rzr.at[r, z], device(xh, y, p, xl, c))

    def onward(cls, i, half, side, p, r, target):
        ref = place(half, side, p, r)
        return remote(ref, ref, ras.at[cls, i], rar.at[cls, i], target)

    pl.semaphore_wait(ready, len(writers))

    @pl.loop(0, PARTS)
    def _(i):
        r, k = i // NZ, i % NZ
        p = near_plane(k)
        for u in range(CHUNK):
            mix(p, r * CHUNK + u)

        @pl.when(k == 0)
        def _():
            pltpu.make_async_copy(rows_of(z, r), place(c, xl, z, r), rzr.at[r, z]).start()

        @pl.when(k > 0)
        def _():
            home(r, k, p).start()

    def project(r, half, side):
        for w in range(2):
            total = jnp.zeros((CHUNK * BLOCK, 256), jnp.float32)
            for pair in range(NZ):
                left = [
                    kbuf[pl.ds((2 * pair + i) * SHARD_BLOCKS + half * HALF_BLOCKS + r * CHUNK, CHUNK)]
                    for i in range(2)
                ]
                right = [kbuf[pl.ds(WEIGHT_AT + ((side * 2 + w) * 2 + i) * 32 + pair * 4, 4)] for i in range(2)]
                total = total + jnp.dot(
                    jnp.concatenate([v.reshape(CHUNK * BLOCK, HEAD_DIM) for v in left], axis=1),
                    jnp.concatenate([v.reshape(256, HEAD_DIM) for v in right], axis=1),
                    preferred_element_type=jnp.float32,
                )
            result = total.astype(jnp.bfloat16)
            for u in range(CHUNK):
                pbuf[tile(r, half, side) + u, :, w * 256:(w + 1) * 256] = result[u * BLOCK:(u + 1) * BLOCK]

    def tile(r, half, side):
        return ((r * NC + half) * 2 + side) * CHUNK

    def result_copy(r, half, side):
        cols = pl.ds(pl.multiple_of(side * 512, 512), 512)
        return pltpu.make_async_copy(
            pbuf.at[pl.ds(tile(r, half, side), CHUNK)],
            out_ref.at[pl.ds(half * HALF_BLOCKS + r * CHUNK, CHUNK), :, cols],
            os.at[r, half * 2 + side],
        )

    @pl.loop(0, PARTS + LAG + NZ)
    def _(step):
        @pl.when(step < PARTS)
        def _():
            r, k = step // NZ, step % NZ
            p = near_plane(k)
            ref = place(c, xl, p, r)
            remote(ref, ref, rzs.at[0, 0], rzr.at[r, p], to_lo).wait_recv()
            onward(0, step, c, xl, p, r, to_lo).start()
            onward(1, step, c, xl, p, r, to_sib).start()

        @pl.when(jnp.logical_and(step >= 2, step < PARTS + 2))
        def _():
            i = step - 2
            r, p = i // NZ, near_plane(i % NZ)
            onward(0, i, c, 1 - xl, p, r, to_lo).wait_recv()
            onward(2, i, c, 1 - xl, p, r, to_sib).start()

        done = step - LAG - NZ

        @pl.when(jnp.logical_and(done >= 0, done % NZ == 0))
        def _():
            @pl.when(done == 0)
            def _():
                @pl.loop(0, NZ)
                def _(g):
                    weight_copy(g).wait()

            @pl.loop(0, NZ)
            def _(k):
                p = near_plane(k)
                onward(1, done + k, 1 - c, xl, p, done // NZ, to_sib).wait_recv()
                onward(2, done + k, 1 - c, 1 - xl, p, done // NZ, to_sib).wait_recv()

        @pl.when(jnp.logical_and(done >= 0, done % 2 == 0))
        def _():
            r, part = done // NZ, (done % NZ) // 2
            project(r, part // 2, part % 2)
            result_copy(r, part // 2, part % 2).start()

    @pl.loop(0, PARTS)
    def _(i):
        r, k = i // NZ, i % NZ
        p = near_plane(k)

        @pl.when(k > 0)
        def _():
            home(r, k, p).wait_send()

        onward(0, i, c, xl, p, r, to_lo).wait_send()
        onward(1, i, c, xl, p, r, to_sib).wait_send()
        onward(2, i, c, 1 - xl, p, r, to_sib).wait_send()

    sends_done(1)

    @pl.loop(0, NZ)
    def _(k):
        for kind in range(3):
            z_each(k, kind, lambda d: d.wait_send(), None)

    for r in range(HALF_BLOCKS // CHUNK):
        for part in range(4):
            result_copy(r, part // 2, part % 2).wait()


def attention_call(table, queries, keys_values, weight):
    anyspace = pl.BlockSpec(memory_space=pl.ANY)
    dma = pltpu.SemaphoreType.DMA
    key_blocks = LINES * LINE_BLOCKS
    return pl.pallas_call(
        attention_kernel,
        out_shape=jax.ShapeDtypeStruct((SHARD_BLOCKS, BLOCK, weight.shape[-1]), jnp.bfloat16),
        in_specs=[pl.BlockSpec(memory_space=pltpu.SMEM), anyspace, anyspace, anyspace],
        out_specs=anyspace,
        scratch_shapes=[
            pltpu.VMEM((key_blocks, BLOCK, HEAD_DIM), jnp.bfloat16),
            pltpu.VMEM((key_blocks, BLOCK, HEAD_DIM), jnp.bfloat16),
            pltpu.VMEM((Q_BLOCKS, BLOCK, HEAD_DIM), jnp.bfloat16),
            pltpu.VMEM((Q_BLOCKS, BLOCK, 512), jnp.bfloat16),
            pltpu.VMEM((Q_BLOCKS, BLOCK, HEAD_DIM), jnp.bfloat16),
            dma((3, NC, NZ)), dma((3, NZ)),
            dma((NCLASS, ITEMS)), dma((NCLASS, ITEMS)),
            dma((ITEMS, LINES)), dma((ITEMS, LINES)),
            dma((HALF_BLOCKS // CHUNK, NZ)), dma((HALF_BLOCKS // CHUNK, NZ)), dma((3, PARTS)), dma((3, PARTS)),
            dma((NZ,)), dma((HALF_BLOCKS // CHUNK, 4)), pltpu.SemaphoreType.REGULAR,
        ],
        compiler_params=pltpu.CompilerParams(
            collective_id=1, has_side_effects=True, vmem_limit_bytes=60 * 1024 * 1024
        ),
        name="block_attention",
    )(table, queries, keys_values, weight)


def body(queries, keys_values, global_ids, rand_ids, out_weight):
    xh, y, z, xl, c = coords()
    width = queries.shape[1]
    lists = rand_ids.reshape(LINES, NZ, NC, HALF_BLOCKS * NRANDOM)
    mine = lax.dynamic_slice(lists, (xh * NY + y, 0, c, 0), (1, NZ, 1, HALF_BLOCKS * NRANDOM)).reshape(-1)
    table = address(jnp.concatenate([mine, global_ids]))
    projected = attention_call(
        table,
        queries.reshape(SHARD_BLOCKS, BLOCK, width),
        keys_values.reshape(2, SHARD_BLOCKS, BLOCK, width),
        out_weight.reshape(-1, BLOCK, out_weight.shape[1]),
    )
    return projected.reshape(ROWS, -1)


def solution(mesh):
    in_specs = (P("seq", "head"), P(None, "seq", "head"), P(), P(), P(None, "head"))
    return jax.shard_map(body, mesh=mesh, in_specs=in_specs, out_specs=P("seq", "head"), check_vma=False)
```

```python
import math

import jax
import jax.numpy as jnp
from jax import lax
from jax.experimental import pallas as pl
from jax.experimental.pallas import tpu as pltpu
from jax.sharding import PartitionSpec as P

HEAD_DIM = 128
BLOCK = 64
NGLOBAL = 2
NRANDOM = 3
MESH = pl.DeviceIdType.MESH

NXH, NY, NZ, NXL, NC = 2, 4, 8, 2, 2
LINES = NXH * NY
SHARD_BLOCKS = 24
ROWS = SHARD_BLOCKS * BLOCK
HALF_BLOCKS = SHARD_BLOCKS // NC
HALF = HALF_BLOCKS * BLOCK
LINE_BLOCKS = NZ * SHARD_BLOCKS
Q_BLOCKS = NZ * HALF_BLOCKS


def coords():
    seq = lax.axis_index("seq")
    head = lax.axis_index("head")
    return seq // (NY * NZ), (seq // NZ) % NY, seq % NZ, head // NC, head % NC


def device(xh, y, z, xl, c):
    return ((xh * NY + y) * NZ + z, xl * NC + c)


def remote(src, dst, send_sem, recv_sem, target):
    return pltpu.make_async_remote_copy(
        src_ref=src, dst_ref=dst, send_sem=send_sem, recv_sem=recv_sem,
        device_id=target, device_id_type=MESH,
    )


def nearest(k):
    return (k % 2) * ((k + 1) // 2) - (1 - k % 2) * (k // 2)


X0, U1, D1, U2, D2, FU, FD, YU, YD, F2, G2, YO = range(12)
NCLASS = 12
FROM_X = (7, 6)
Z_LEAD = 2
ITEMS = 2 * NZ
CHUNK = 4
PARTS = NZ * HALF_BLOCKS // CHUNK
FORWARD = 6
LAG = 3
WEIGHT_AT = 512
DELAY = (0, 0, 2, 4, 6)
SCORES_FROM = NZ + DELAY[4]
SCALE = math.log2(math.e) / HEAD_DIM**0.5


def address(block):
    shard, offset = block // SHARD_BLOCKS, block % SHARD_BLOCKS
    line, plane = shard // NZ, shard % NZ
    return ((line * NC + offset // HALF_BLOCKS) * NZ + plane) * HALF_BLOCKS + offset % HALF_BLOCKS


def attention_kernel(
    table, q_ref, kv_ref, w_ref, out_ref, kbuf, vbuf, qbuf, pbuf, obuf,
    zs, zr, cs, cr, bs, br, rzs, rzr, ras, rar, ws, os, ready,
):
    xh, y, z, xl, c = coords()
    line = xh * NY + y
    up, down, opp = (y + 1) % NY, (y + NY - 1) % NY, (y + 2) % NY
    ox = 1 - xh
    to_x, to_up, to_down = device(ox, y, z, xl, c), device(xh, up, z, xl, c), device(xh, down, z, xl, c)
    to_sib, to_lo = device(xh, y, z, xl, 1 - c), device(xh, y, z, 1 - xl, c)
    bufs = (kbuf, vbuf)

    barrier = pltpu.get_barrier_semaphore()
    friends = [
        device(xh, y, (z + dz) % NZ, xl, (c + dc) % NC)
        for dz in range(NZ) for dc in range(NC) if dz or dc
    ] + [to_x, to_up, to_down, to_lo]
    for friend in friends:
        pl.semaphore_signal(barrier, inc=1, device_id=friend, device_id_type=MESH)
    pl.semaphore_wait(barrier, len(friends))

    def piece(kv, ln, half, p):
        return bufs[kv].at[pl.ds(((ln * NC + half) * NZ + p) * HALF_BLOCKS, HALF_BLOCKS)]

    def near_plane(k):
        return (z + nearest(k) + NZ) % NZ

    def z_parts(t, kind, half):
        cols = pl.ds(pl.multiple_of((t - 4 * c) * HEAD_DIM, HEAD_DIM), HEAD_DIM)
        rows = pl.ds(half * HALF_BLOCKS, HALF_BLOCKS)
        if kind == 2:
            return q_ref.at[rows, :, cols], qbuf.at[pl.ds(z * HALF_BLOCKS, HALF_BLOCKS)]
        return kv_ref.at[kind, rows, :, cols], piece(kind, line, half, z)

    def z_each(k, kind, remote_fn, local_fn):
        t = near_plane(k)

        @pl.when(t // 4 == c)
        def _():
            for half in range(NC):
                src, dst = z_parts(t, kind, half)
                mine = jnp.logical_and(t == z, c == half)
                if local_fn is not None:
                    @pl.when(mine)
                    def _():
                        local_fn(pltpu.make_async_copy(src, dst, zr.at[kind, z]))

                @pl.when(jnp.logical_not(mine))
                def _():
                    remote_fn(remote(src, dst, zs.at[kind, half, k], zr.at[kind, z], device(xh, y, t, xl, half)))

    def z_start(k, kind):
        z_each(k, kind, lambda d: d.start(), lambda d: d.start())

    @pl.loop(0, Z_LEAD)
    def _(k):
        z_start(k, 0)

    H = HALF_BLOCKS // 2

    def at(xx, yy):
        return xx * NY + yy

    def routes(kv):
        m = FROM_X[kv]
        h = (m + 1) // 2
        rest = (m, HALF_BLOCKS - m)
        return {
            X0: (line, to_x, (0, HALF_BLOCKS), at(ox, y)),
            U1: (line, to_up, (0, HALF_BLOCKS), at(xh, down)),
            D1: (line, to_down, (0, HALF_BLOCKS), at(xh, up)),
            U2: (at(ox, y), to_up, (0, m), at(ox, down)),
            D2: (at(ox, y), to_down, (0, m), at(ox, up)),
            FU: (at(xh, down), to_up, (0, H), at(xh, opp)),
            FD: (at(xh, up), to_down, (H, H), at(xh, opp)),
            YU: (at(xh, down), to_x, rest, at(ox, down)),
            YD: (at(xh, up), to_x, rest, at(ox, up)),
            F2: (at(ox, down), to_up, (0, h), at(ox, opp)),
            G2: (at(ox, up), to_down, (h, m - h), at(ox, opp)),
            YO: (at(xh, opp), to_x, rest, at(ox, opp)),
        }

    def copy(cls, e, p, kv, ln, target, span):
        ref = piece(kv, ln, c, p).at[pl.ds(*span)]
        return remote(ref, ref, cs.at[cls, e], cr.at[cls, e], target)

    def sib(e, p, kv, ln, half):
        ref = piece(kv, ln, half, p)
        return remote(ref, ref, bs.at[e, ln], br.at[e, ln], to_sib)

    def stages(kv, k, p, stage):
        e = kv * NZ + k
        classes = routes(kv)

        def send(*names):
            for cls in names:
                ln, target, span, _ = classes[cls]
                copy(cls, e, p, kv, ln, target, span).start()

        def wait(*names):
            for cls in names:
                _, target, span, ln = classes[cls]
                copy(cls, e, p, kv, ln, target, span).wait_recv()

        def share(*lines):
            for ln in lines:
                sib(e, p, kv, ln, c).start()

        if stage == 1:
            ref = piece(kv, line, c, p)
            remote(ref, ref, zs.at[kv, 0, 0], zr.at[kv, p], to_x).wait_recv()
            send(X0, U1, D1)
            share(line)
        elif stage == 2:
            wait(X0)
            send(U2, D2)
            wait(U1)
            send(YU, FU)
            wait(D1)
            send(YD, FD)
            share(at(ox, y), at(xh, down), at(xh, up))
        elif stage == 3:
            wait(U2)
            send(F2)
            wait(D2)
            send(G2)
            wait(FU, FD)
            send(YO)
            share(at(xh, opp))
        else:
            wait(YU, YD)
            share(at(ox, down), at(ox, up))
            wait(F2, G2, YO)
            share(at(ox, opp))

    def sib_received(kv):
        @pl.loop(0, NZ)
        def _(k):
            p = near_plane(k)

            @pl.loop(0, LINES)
            def _(ln):
                sib(kv * NZ + k, p, kv, ln, 1 - c).wait_recv()

    column = lax.broadcasted_iota(jnp.int32, (1, 512), 1)
    globals_at = Q_BLOCKS * NRANDOM

    def listed(buf, n, block):
        last_block = LINES * LINE_BLOCKS - 1
        spots = [
            address(jnp.maximum(block - 1, 0)), address(block), address(jnp.minimum(block + 1, last_block)),
        ] + [table[n * NRANDOM + r] for r in range(NRANDOM)] + [table[globals_at + g] for g in range(NGLOBAL)]
        return jnp.concatenate([buf[s] for s in spots], axis=0)

    def doc_block(plane, o):
        return line * LINE_BLOCKS + plane * SHARD_BLOCKS + c * HALF_BLOCKS + o

    def weigh(plane, o):
        n, block = plane * HALF_BLOCKS + o, doc_block(plane, o)
        first = jnp.logical_and(block == 0, column < BLOCK)
        last = jnp.logical_and(
            block == LINES * LINE_BLOCKS - 1, jnp.logical_and(column >= 2 * BLOCK, column < 3 * BLOCK)
        )
        bias = jnp.where(jnp.logical_or(first, last), -jnp.inf, 0.0).astype(jnp.float32)
        scores = lax.dot_general(
            qbuf[n], listed(kbuf, n, block), (((1,), (1,)), ((), ())), preferred_element_type=jnp.float32
        )
        scores = scores * SCALE + bias
        powers = jnp.exp2(scores - jnp.max(scores, axis=1, keepdims=True))
        pbuf[n] = (powers * (1.0 / jnp.sum(powers, axis=1, keepdims=True))).astype(jnp.bfloat16)

    def mix(plane, o):
        n, block = plane * HALF_BLOCKS + o, doc_block(plane, o)
        mixed = jnp.dot(pbuf[n], listed(vbuf, n, block), preferred_element_type=jnp.float32)
        obuf[n] = mixed.astype(jnp.bfloat16)

    def weight_copy(g):
        cols = pl.ds(pl.multiple_of(g * HEAD_DIM, HEAD_DIM), HEAD_DIM)
        return pltpu.make_async_copy(w_ref.at[:, :, cols], kbuf.at[pl.ds(WEIGHT_AT + g * 32, 32)], ws.at[g])

    writers = [device(xh, y, (z + dz) % NZ, xl, c) for dz in range(1, NZ)] + [to_lo, to_sib]

    def sends_done(kv):
        @pl.loop(0, NZ)
        def _(k):
            p = near_plane(k)
            e = kv * NZ + k
            for cls, (ln, target, span, _) in routes(kv).items():
                copy(cls, e, p, kv, ln, target, span).wait_send()

            @pl.loop(0, LINES)
            def _(ln):
                sib(e, p, kv, ln, c).wait_send()

    def blocks_of(plane, fn):
        @pl.loop(0, HALF_BLOCKS // 4)
        def _(m):
            for u in range(4):
                fn(plane, m * 4 + u)

    @pl.loop(0, ITEMS + DELAY[4])
    def _(step):
        for kind, lag in ((0, -Z_LEAD), (1, 5), (2, 6)):
            @pl.when(jnp.logical_and(step >= max(lag, 0), step < NZ + lag))
            def _():
                z_start(step - lag, kind)

        for stage in (4, 3, 2, 1):
            e = step - DELAY[stage]
            for kv in range(2):
                @pl.when(jnp.logical_and(e >= kv * NZ, e < (kv + 1) * NZ))
                def _():
                    k = e - kv * NZ
                    p = near_plane(k)
                    stages(kv, k, p, stage)

        @pl.when(step == SCORES_FROM)
        def _():
            sib_received(0)

            @pl.loop(0, NZ)
            def _(p):
                ref = qbuf.at[pl.ds(p * HALF_BLOCKS, HALF_BLOCKS)]
                remote(ref, ref, zs.at[2, 0, 0], zr.at[2, p], to_x).wait_recv()

        @pl.when(jnp.logical_and(step >= SCORES_FROM, step < SCORES_FROM + NZ // 2))
        def _():
            for u in range(2):
                blocks_of(2 * (step - SCORES_FROM) + u, weigh)

        @pl.when(step == SCORES_FROM + NZ // 2)
        def _():
            sends_done(0)

            @pl.loop(0, NZ)
            def _(g):
                weight_copy(g).start()

            for writer in writers:
                pl.semaphore_signal(ready, inc=1, device_id=writer, device_id_type=MESH)

    sib_received(1)

    def place(half, side, plane, r):
        return kbuf.at[pl.ds((side * NZ + plane) * SHARD_BLOCKS + half * HALF_BLOCKS + r * CHUNK, CHUNK)]

    def rows_of(p, r):
        return obuf.at[pl.ds(p * HALF_BLOCKS + r * CHUNK, CHUNK)]

    def home(r, k, p):
        return remote(rows_of(p, r), place(c, xl, z, r), rzs.at[r, k], rzr.at[r, z], device(xh, y, p, xl, c))

    def onward(cls, i, half, side, p, r, target):
        ref = place(half, side, p, r)
        return remote(ref, ref, ras.at[cls, i], rar.at[cls, i], target)

    pl.semaphore_wait(ready, len(writers))

    def project(r, half, side):
        for w in range(2):
            total = jnp.zeros((CHUNK * BLOCK, 256), jnp.float32)
            for pair in range(NZ):
                left = [
                    kbuf[pl.ds((2 * pair + i) * SHARD_BLOCKS + half * HALF_BLOCKS + r * CHUNK, CHUNK)]
                    for i in range(2)
                ]
                right = [kbuf[pl.ds(WEIGHT_AT + ((side * 2 + w) * 2 + i) * 32 + pair * 4, 4)] for i in range(2)]
                total = total + jnp.dot(
                    jnp.concatenate([v.reshape(CHUNK * BLOCK, HEAD_DIM) for v in left], axis=1),
                    jnp.concatenate([v.reshape(256, HEAD_DIM) for v in right], axis=1),
                    preferred_element_type=jnp.float32,
                )
            result = total.astype(jnp.bfloat16)
            for u in range(CHUNK):
                pbuf[tile(r, half, side) + u, :, w * 256:(w + 1) * 256] = result[u * BLOCK:(u + 1) * BLOCK]

    def tile(r, half, side):
        return (half * 2 + side) * HALF_BLOCKS + r * CHUNK

    def result_copy(r, half, side):
        cols = pl.ds(pl.multiple_of(side * 512, 512), 512)
        return pltpu.make_async_copy(
            pbuf.at[pl.ds(tile(r, half, side), CHUNK)],
            out_ref.at[pl.ds(half * HALF_BLOCKS + r * CHUNK, CHUNK), :, cols],
            os.at[r, half * 2 + side],
        )

    @pl.loop(0, PARTS + FORWARD + LAG + NZ)
    def _(tick):
        @pl.when(tick < PARTS)
        def _():
            r, k = tick // NZ, tick % NZ
            p = near_plane(k)
            for u in range(CHUNK):
                mix(p, r * CHUNK + u)

            @pl.when(k == 0)
            def _():
                pltpu.make_async_copy(rows_of(z, r), place(c, xl, z, r), rzr.at[r, z]).start()

            @pl.when(k > 0)
            def _():
                home(r, k, p).start()

        step = tick - FORWARD

        @pl.when(jnp.logical_and(step >= 0, step < PARTS))
        def _():
            r, k = step // NZ, step % NZ
            p = near_plane(k)
            ref = place(c, xl, p, r)
            remote(ref, ref, rzs.at[0, 0], rzr.at[r, p], to_lo).wait_recv()
            onward(0, step, c, xl, p, r, to_lo).start()
            onward(1, step, c, xl, p, r, to_sib).start()

        @pl.when(jnp.logical_and(step >= 2, step < PARTS + 2))
        def _():
            i = step - 2
            r, p = i // NZ, near_plane(i % NZ)
            onward(0, i, c, 1 - xl, p, r, to_lo).wait_recv()
            onward(2, i, c, 1 - xl, p, r, to_sib).start()

        done = step - LAG - NZ

        @pl.when(jnp.logical_and(done >= 0, done % NZ == 0))
        def _():
            @pl.when(done == 0)
            def _():
                @pl.loop(0, NZ)
                def _(g):
                    weight_copy(g).wait()

            @pl.loop(0, NZ)
            def _(k):
                p = near_plane(k)
                onward(1, done + k, 1 - c, xl, p, done // NZ, to_sib).wait_recv()
                onward(2, done + k, 1 - c, 1 - xl, p, done // NZ, to_sib).wait_recv()

        @pl.when(jnp.logical_and(done >= 0, done % 2 == 0))
        def _():
            r, part = done // NZ, (done % NZ) // 2
            project(r, part // 2, part % 2)
            result_copy(r, part // 2, part % 2).start()

    @pl.loop(0, PARTS)
    def _(i):
        r, k = i // NZ, i % NZ
        p = near_plane(k)

        @pl.when(k > 0)
        def _():
            home(r, k, p).wait_send()

        onward(0, i, c, xl, p, r, to_lo).wait_send()
        onward(1, i, c, xl, p, r, to_sib).wait_send()
        onward(2, i, c, 1 - xl, p, r, to_sib).wait_send()

    sends_done(1)

    @pl.loop(0, NZ)
    def _(k):
        for kind in range(3):
            z_each(k, kind, lambda d: d.wait_send(), None)

    for r in range(HALF_BLOCKS // CHUNK):
        for part in range(4):
            result_copy(r, part // 2, part % 2).wait()


def attention_call(table, queries, keys_values, weight):
    anyspace = pl.BlockSpec(memory_space=pl.ANY)
    dma = pltpu.SemaphoreType.DMA
    key_blocks = LINES * LINE_BLOCKS
    return pl.pallas_call(
        attention_kernel,
        out_shape=jax.ShapeDtypeStruct((SHARD_BLOCKS, BLOCK, weight.shape[-1]), jnp.bfloat16),
        in_specs=[pl.BlockSpec(memory_space=pltpu.SMEM), anyspace, anyspace, anyspace],
        out_specs=anyspace,
        scratch_shapes=[
            pltpu.VMEM((key_blocks, BLOCK, HEAD_DIM), jnp.bfloat16),
            pltpu.VMEM((key_blocks, BLOCK, HEAD_DIM), jnp.bfloat16),
            pltpu.VMEM((Q_BLOCKS, BLOCK, HEAD_DIM), jnp.bfloat16),
            pltpu.VMEM((Q_BLOCKS, BLOCK, 512), jnp.bfloat16),
            pltpu.VMEM((Q_BLOCKS, BLOCK, HEAD_DIM), jnp.bfloat16),
            dma((3, NC, NZ)), dma((3, NZ)),
            dma((NCLASS, ITEMS)), dma((NCLASS, ITEMS)),
            dma((ITEMS, LINES)), dma((ITEMS, LINES)),
            dma((HALF_BLOCKS // CHUNK, NZ)), dma((HALF_BLOCKS // CHUNK, NZ)), dma((3, PARTS)), dma((3, PARTS)),
            dma((NZ,)), dma((HALF_BLOCKS // CHUNK, 4)), pltpu.SemaphoreType.REGULAR,
        ],
        compiler_params=pltpu.CompilerParams(
            collective_id=1, has_side_effects=True, vmem_limit_bytes=60 * 1024 * 1024
        ),
        name="block_attention",
    )(table, queries, keys_values, weight)


def body(queries, keys_values, global_ids, rand_ids, out_weight):
    xh, y, z, xl, c = coords()
    width = queries.shape[1]
    lists = rand_ids.reshape(LINES, NZ, NC, HALF_BLOCKS * NRANDOM)
    mine = lax.dynamic_slice(lists, (xh * NY + y, 0, c, 0), (1, NZ, 1, HALF_BLOCKS * NRANDOM)).reshape(-1)
    table = address(jnp.concatenate([mine, global_ids]))
    projected = attention_call(
        table,
        queries.reshape(SHARD_BLOCKS, BLOCK, width),
        keys_values.reshape(2, SHARD_BLOCKS, BLOCK, width),
        out_weight.reshape(-1, BLOCK, out_weight.shape[1]),
    )
    return projected.reshape(ROWS, -1)


def solution(mesh):
    in_specs = (P("seq", "head"), P(None, "seq", "head"), P(), P(), P(None, "head"))
    return jax.shard_map(body, mesh=mesh, in_specs=in_specs, out_specs=P("seq", "head"), check_vma=False)
```

```python
import math

import jax
import jax.numpy as jnp
from jax import lax
from jax.experimental import pallas as pl
from jax.experimental.pallas import tpu as pltpu
from jax.sharding import PartitionSpec as P

HEAD_DIM = 128
BLOCK = 64
NGLOBAL = 2
NRANDOM = 3
MESH = pl.DeviceIdType.MESH

NXH, NY, NZ, NXL, NC = 2, 4, 8, 2, 2
LINES = NXH * NY
SHARD_BLOCKS = 24
ROWS = SHARD_BLOCKS * BLOCK
HALF_BLOCKS = SHARD_BLOCKS // NC
HALF = HALF_BLOCKS * BLOCK
LINE_BLOCKS = NZ * SHARD_BLOCKS
Q_BLOCKS = NZ * HALF_BLOCKS


def coords():
    seq = lax.axis_index("seq")
    head = lax.axis_index("head")
    return seq // (NY * NZ), (seq // NZ) % NY, seq % NZ, head // NC, head % NC


def device(xh, y, z, xl, c):
    return ((xh * NY + y) * NZ + z, xl * NC + c)


def remote(src, dst, send_sem, recv_sem, target):
    return pltpu.make_async_remote_copy(
        src_ref=src, dst_ref=dst, send_sem=send_sem, recv_sem=recv_sem,
        device_id=target, device_id_type=MESH,
    )


def nearest(k):
    return (k % 2) * ((k + 1) // 2) - (1 - k % 2) * (k // 2)


X0, U1, D1, U2, D2, FU, FD, YU, YD, F2, G2, YO = range(12)
NCLASS = 12
FROM_X = (7, 6)
Z_LEAD = 2
ITEMS = 2 * NZ
CHUNK = 4
PARTS = NZ * HALF_BLOCKS // CHUNK
FORWARD = 6
RELAY = 5
LAG = 6
WEIGHT_AT = 512
DELAY = (0, 0, 2, 4, 6)
SCORES_FROM = NZ + DELAY[4]
SCALE = math.log2(math.e) / HEAD_DIM**0.5


def address(block):
    shard, offset = block // SHARD_BLOCKS, block % SHARD_BLOCKS
    line, plane = shard // NZ, shard % NZ
    return ((line * NC + offset // HALF_BLOCKS) * NZ + plane) * HALF_BLOCKS + offset % HALF_BLOCKS


def attention_kernel(
    table, q_ref, kv_ref, w_ref, out_ref, kbuf, vbuf, qbuf, pbuf, obuf,
    zs, zr, cs, cr, bs, br, rzs, rzr, ras, rar, ws, os, ready,
):
    xh, y, z, xl, c = coords()
    line = xh * NY + y
    up, down, opp = (y + 1) % NY, (y + NY - 1) % NY, (y + 2) % NY
    ox = 1 - xh
    to_x, to_up, to_down = device(ox, y, z, xl, c), device(xh, up, z, xl, c), device(xh, down, z, xl, c)
    to_sib, to_lo = device(xh, y, z, xl, 1 - c), device(xh, y, z, 1 - xl, c)
    bufs = (kbuf, vbuf)

    barrier = pltpu.get_barrier_semaphore()
    friends = [
        device(xh, y, (z + dz) % NZ, xl, (c + dc) % NC)
        for dz in range(NZ) for dc in range(NC) if dz or dc
    ] + [to_x, to_up, to_down, to_lo]
    for friend in friends:
        pl.semaphore_signal(barrier, inc=1, device_id=friend, device_id_type=MESH)
    pl.semaphore_wait(barrier, len(friends))

    def piece(kv, ln, half, p):
        return bufs[kv].at[pl.ds(((ln * NC + half) * NZ + p) * HALF_BLOCKS, HALF_BLOCKS)]

    def near_plane(k):
        return (z + nearest(k) + NZ) % NZ

    def z_parts(t, kind, half):
        cols = pl.ds(pl.multiple_of((t - 4 * c) * HEAD_DIM, HEAD_DIM), HEAD_DIM)
        rows = pl.ds(half * HALF_BLOCKS, HALF_BLOCKS)
        if kind == 2:
            return q_ref.at[rows, :, cols], qbuf.at[pl.ds(z * HALF_BLOCKS, HALF_BLOCKS)]
        return kv_ref.at[kind, rows, :, cols], piece(kind, line, half, z)

    def z_each(k, kind, remote_fn, local_fn):
        t = near_plane(k)

        @pl.when(t // 4 == c)
        def _():
            for half in range(NC):
                src, dst = z_parts(t, kind, half)
                mine = jnp.logical_and(t == z, c == half)
                if local_fn is not None:
                    @pl.when(mine)
                    def _():
                        local_fn(pltpu.make_async_copy(src, dst, zr.at[kind, z]))

                @pl.when(jnp.logical_not(mine))
                def _():
                    remote_fn(remote(src, dst, zs.at[kind, half, k], zr.at[kind, z], device(xh, y, t, xl, half)))

    def z_start(k, kind):
        z_each(k, kind, lambda d: d.start(), lambda d: d.start())

    @pl.loop(0, Z_LEAD)
    def _(k):
        z_start(k, 0)

    H = HALF_BLOCKS // 2

    def at(xx, yy):
        return xx * NY + yy

    def routes(kv):
        m = FROM_X[kv]
        h = (m + 1) // 2
        rest = (m, HALF_BLOCKS - m)
        return {
            X0: (line, to_x, (0, HALF_BLOCKS), at(ox, y)),
            U1: (line, to_up, (0, HALF_BLOCKS), at(xh, down)),
            D1: (line, to_down, (0, HALF_BLOCKS), at(xh, up)),
            U2: (at(ox, y), to_up, (0, m), at(ox, down)),
            D2: (at(ox, y), to_down, (0, m), at(ox, up)),
            FU: (at(xh, down), to_up, (0, H), at(xh, opp)),
            FD: (at(xh, up), to_down, (H, H), at(xh, opp)),
            YU: (at(xh, down), to_x, rest, at(ox, down)),
            YD: (at(xh, up), to_x, rest, at(ox, up)),
            F2: (at(ox, down), to_up, (0, h), at(ox, opp)),
            G2: (at(ox, up), to_down, (h, m - h), at(ox, opp)),
            YO: (at(xh, opp), to_x, rest, at(ox, opp)),
        }

    def copy(cls, e, p, kv, ln, target, span):
        ref = piece(kv, ln, c, p).at[pl.ds(*span)]
        return remote(ref, ref, cs.at[cls, e], cr.at[cls, e], target)

    def sib(e, p, kv, ln, half):
        ref = piece(kv, ln, half, p)
        return remote(ref, ref, bs.at[e, ln], br.at[e, ln], to_sib)

    def stages(kv, k, p, stage):
        e = kv * NZ + k
        classes = routes(kv)

        def send(*names):
            for cls in names:
                ln, target, span, _ = classes[cls]
                copy(cls, e, p, kv, ln, target, span).start()

        def wait(*names):
            for cls in names:
                _, target, span, ln = classes[cls]
                copy(cls, e, p, kv, ln, target, span).wait_recv()

        def share(*lines):
            for ln in lines:
                sib(e, p, kv, ln, c).start()

        if stage == 1:
            ref = piece(kv, line, c, p)
            remote(ref, ref, zs.at[kv, 0, 0], zr.at[kv, p], to_x).wait_recv()
            send(X0, U1, D1)
            share(line)
        elif stage == 2:
            wait(X0)
            send(U2, D2)
            wait(U1)
            send(YU, FU)
            wait(D1)
            send(YD, FD)
            share(at(ox, y), at(xh, down), at(xh, up))
        elif stage == 3:
            wait(U2)
            send(F2)
            wait(D2)
            send(G2)
            wait(FU, FD)
            send(YO)
            share(at(xh, opp))
        else:
            wait(YU, YD)
            share(at(ox, down), at(ox, up))
            wait(F2, G2, YO)
            share(at(ox, opp))

    def sib_received(kv):
        @pl.loop(0, NZ)
        def _(k):
            p = near_plane(k)

            @pl.loop(0, LINES)
            def _(ln):
                sib(kv * NZ + k, p, kv, ln, 1 - c).wait_recv()

    column = lax.broadcasted_iota(jnp.int32, (1, 512), 1)
    globals_at = Q_BLOCKS * NRANDOM

    def listed(buf, n, block):
        last_block = LINES * LINE_BLOCKS - 1
        spots = [
            address(jnp.maximum(block - 1, 0)), address(block), address(jnp.minimum(block + 1, last_block)),
        ] + [table[n * NRANDOM + r] for r in range(NRANDOM)] + [table[globals_at + g] for g in range(NGLOBAL)]
        return jnp.concatenate([buf[s] for s in spots], axis=0)

    def doc_block(plane, o):
        return line * LINE_BLOCKS + plane * SHARD_BLOCKS + c * HALF_BLOCKS + o

    def weigh(plane, o):
        n, block = plane * HALF_BLOCKS + o, doc_block(plane, o)
        first = jnp.logical_and(block == 0, column < BLOCK)
        last = jnp.logical_and(
            block == LINES * LINE_BLOCKS - 1, jnp.logical_and(column >= 2 * BLOCK, column < 3 * BLOCK)
        )
        bias = jnp.where(jnp.logical_or(first, last), -jnp.inf, 0.0).astype(jnp.float32)
        scores = lax.dot_general(
            qbuf[n], listed(kbuf, n, block), (((1,), (1,)), ((), ())), preferred_element_type=jnp.float32
        )
        scores = scores * SCALE + bias
        powers = jnp.exp2(scores - jnp.max(scores, axis=1, keepdims=True))
        pbuf[n] = (powers * (1.0 / jnp.sum(powers, axis=1, keepdims=True))).astype(jnp.bfloat16)

    def mix(plane, o):
        n, block = plane * HALF_BLOCKS + o, doc_block(plane, o)
        mixed = jnp.dot(pbuf[n], listed(vbuf, n, block), preferred_element_type=jnp.float32)
        obuf[n] = mixed.astype(jnp.bfloat16)

    def weight_copy(g):
        cols = pl.ds(pl.multiple_of(g * HEAD_DIM, HEAD_DIM), HEAD_DIM)
        return pltpu.make_async_copy(w_ref.at[:, :, cols], kbuf.at[pl.ds(WEIGHT_AT + g * 32, 32)], ws.at[g])

    writers = [device(xh, y, (z + dz) % NZ, xl, c) for dz in range(1, NZ)] + [to_lo, to_sib]

    def sends_done(kv):
        @pl.loop(0, NZ)
        def _(k):
            p = near_plane(k)
            e = kv * NZ + k
            for cls, (ln, target, span, _) in routes(kv).items():
                copy(cls, e, p, kv, ln, target, span).wait_send()

            @pl.loop(0, LINES)
            def _(ln):
                sib(e, p, kv, ln, c).wait_send()

    def blocks_of(plane, fn):
        @pl.loop(0, HALF_BLOCKS // 4)
        def _(m):
            for u in range(4):
                fn(plane, m * 4 + u)

    @pl.loop(0, ITEMS + DELAY[4])
    def _(step):
        for kind, lag in ((0, -Z_LEAD), (1, 5), (2, 6)):
            @pl.when(jnp.logical_and(step >= max(lag, 0), step < NZ + lag))
            def _():
                z_start(step - lag, kind)

        for stage in (4, 3, 2, 1):
            e = step - DELAY[stage]
            for kv in range(2):
                @pl.when(jnp.logical_and(e >= kv * NZ, e < (kv + 1) * NZ))
                def _():
                    k = e - kv * NZ
                    p = near_plane(k)
                    stages(kv, k, p, stage)

        @pl.when(step == SCORES_FROM)
        def _():
            sib_received(0)

            @pl.loop(0, NZ)
            def _(p):
                ref = qbuf.at[pl.ds(p * HALF_BLOCKS, HALF_BLOCKS)]
                remote(ref, ref, zs.at[2, 0, 0], zr.at[2, p], to_x).wait_recv()

        @pl.when(jnp.logical_and(step >= SCORES_FROM, step < SCORES_FROM + NZ // 2))
        def _():
            for u in range(2):
                blocks_of(2 * (step - SCORES_FROM) + u, weigh)

        @pl.when(step == SCORES_FROM + NZ // 2)
        def _():
            sends_done(0)

            @pl.loop(0, NZ)
            def _(g):
                weight_copy(g).start()

            for writer in writers:
                pl.semaphore_signal(ready, inc=1, device_id=writer, device_id_type=MESH)

    sib_received(1)

    def place(half, side, plane, r):
        return kbuf.at[pl.ds((side * NZ + plane) * SHARD_BLOCKS + half * HALF_BLOCKS + r * CHUNK, CHUNK)]

    def rows_of(p, r):
        return obuf.at[pl.ds(p * HALF_BLOCKS + r * CHUNK, CHUNK)]

    def home(r, k, p):
        return remote(rows_of(p, r), place(c, xl, z, r), rzs.at[r, k], rzr.at[r, z], device(xh, y, p, xl, c))

    def onward(cls, i, half, side, p, r, target):
        ref = place(half, side, p, r)
        return remote(ref, ref, ras.at[cls, i], rar.at[cls, i], target)

    pl.semaphore_wait(ready, len(writers))

    def project(r, half, side):
        for w in range(2):
            total = jnp.zeros((CHUNK * BLOCK, 256), jnp.float32)
            for pair in range(NZ):
                left = [
                    kbuf[pl.ds((2 * pair + i) * SHARD_BLOCKS + half * HALF_BLOCKS + r * CHUNK, CHUNK)]
                    for i in range(2)
                ]
                right = [kbuf[pl.ds(WEIGHT_AT + ((side * 2 + w) * 2 + i) * 32 + pair * 4, 4)] for i in range(2)]
                total = total + jnp.dot(
                    jnp.concatenate([v.reshape(CHUNK * BLOCK, HEAD_DIM) for v in left], axis=1),
                    jnp.concatenate([v.reshape(256, HEAD_DIM) for v in right], axis=1),
                    preferred_element_type=jnp.float32,
                )
            result = total.astype(jnp.bfloat16)
            for u in range(CHUNK):
                pbuf[tile(r, half, side) + u, :, w * 256:(w + 1) * 256] = result[u * BLOCK:(u + 1) * BLOCK]

    def tile(r, half, side):
        return (half * 2 + side) * HALF_BLOCKS + r * CHUNK

    def result_copy(r, half, side):
        cols = pl.ds(pl.multiple_of(side * 512, 512), 512)
        return pltpu.make_async_copy(
            pbuf.at[pl.ds(tile(r, half, side), CHUNK)],
            out_ref.at[pl.ds(half * HALF_BLOCKS + r * CHUNK, CHUNK), :, cols],
            os.at[r, half * 2 + side],
        )

    @pl.loop(0, PARTS + FORWARD + LAG + NZ)
    def _(tick):
        @pl.when(tick < PARTS)
        def _():
            r, k = tick // NZ, tick % NZ
            p = near_plane(k)
            for u in range(CHUNK):
                mix(p, r * CHUNK + u)

            @pl.when(k == 0)
            def _():
                pltpu.make_async_copy(rows_of(z, r), place(c, xl, z, r), rzr.at[r, z]).start()

            @pl.when(k > 0)
            def _():
                home(r, k, p).start()

        step = tick - FORWARD

        @pl.when(jnp.logical_and(step >= 0, step < PARTS))
        def _():
            r, k = step // NZ, step % NZ
            p = near_plane(k)
            ref = place(c, xl, p, r)
            remote(ref, ref, rzs.at[0, 0], rzr.at[r, p], to_lo).wait_recv()
            onward(0, step, c, xl, p, r, to_lo).start()
            onward(1, step, c, xl, p, r, to_sib).start()

        @pl.when(jnp.logical_and(step >= RELAY, step < PARTS + RELAY))
        def _():
            i = step - RELAY
            r, p = i // NZ, near_plane(i % NZ)
            onward(0, i, c, 1 - xl, p, r, to_lo).wait_recv()
            onward(2, i, c, 1 - xl, p, r, to_sib).start()

        done = step - LAG - NZ

        @pl.when(jnp.logical_and(done >= 0, done % NZ == 0))
        def _():
            @pl.when(done == 0)
            def _():
                @pl.loop(0, NZ)
                def _(g):
                    weight_copy(g).wait()

            @pl.loop(0, NZ)
            def _(k):
                p = near_plane(k)
                onward(1, done + k, 1 - c, xl, p, done // NZ, to_sib).wait_recv()
                onward(2, done + k, 1 - c, 1 - xl, p, done // NZ, to_sib).wait_recv()

        @pl.when(jnp.logical_and(done >= 0, done % 2 == 0))
        def _():
            r, part = done // NZ, (done % NZ) // 2
            project(r, part // 2, part % 2)
            result_copy(r, part // 2, part % 2).start()

    @pl.loop(0, PARTS)
    def _(i):
        r, k = i // NZ, i % NZ
        p = near_plane(k)

        @pl.when(k > 0)
        def _():
            home(r, k, p).wait_send()

        onward(0, i, c, xl, p, r, to_lo).wait_send()
        onward(1, i, c, xl, p, r, to_sib).wait_send()
        onward(2, i, c, 1 - xl, p, r, to_sib).wait_send()

    sends_done(1)

    @pl.loop(0, NZ)
    def _(k):
        for kind in range(3):
            z_each(k, kind, lambda d: d.wait_send(), None)

    for r in range(HALF_BLOCKS // CHUNK):
        for part in range(4):
            result_copy(r, part // 2, part % 2).wait()


def attention_call(table, queries, keys_values, weight):
    anyspace = pl.BlockSpec(memory_space=pl.ANY)
    dma = pltpu.SemaphoreType.DMA
    key_blocks = LINES * LINE_BLOCKS
    return pl.pallas_call(
        attention_kernel,
        out_shape=jax.ShapeDtypeStruct((SHARD_BLOCKS, BLOCK, weight.shape[-1]), jnp.bfloat16),
        in_specs=[pl.BlockSpec(memory_space=pltpu.SMEM), anyspace, anyspace, anyspace],
        out_specs=anyspace,
        scratch_shapes=[
            pltpu.VMEM((key_blocks, BLOCK, HEAD_DIM), jnp.bfloat16),
            pltpu.VMEM((key_blocks, BLOCK, HEAD_DIM), jnp.bfloat16),
            pltpu.VMEM((Q_BLOCKS, BLOCK, HEAD_DIM), jnp.bfloat16),
            pltpu.VMEM((Q_BLOCKS, BLOCK, 512), jnp.bfloat16),
            pltpu.VMEM((Q_BLOCKS, BLOCK, HEAD_DIM), jnp.bfloat16),
            dma((3, NC, NZ)), dma((3, NZ)),
            dma((NCLASS, ITEMS)), dma((NCLASS, ITEMS)),
            dma((ITEMS, LINES)), dma((ITEMS, LINES)),
            dma((HALF_BLOCKS // CHUNK, NZ)), dma((HALF_BLOCKS // CHUNK, NZ)), dma((3, PARTS)), dma((3, PARTS)),
            dma((NZ,)), dma((HALF_BLOCKS // CHUNK, 4)), pltpu.SemaphoreType.REGULAR,
        ],
        compiler_params=pltpu.CompilerParams(
            collective_id=1, has_side_effects=True, vmem_limit_bytes=60 * 1024 * 1024
        ),
        name="block_attention",
    )(table, queries, keys_values, weight)


def body(queries, keys_values, global_ids, rand_ids, out_weight):
    xh, y, z, xl, c = coords()
    width = queries.shape[1]
    lists = rand_ids.reshape(LINES, NZ, NC, HALF_BLOCKS * NRANDOM)
    mine = lax.dynamic_slice(lists, (xh * NY + y, 0, c, 0), (1, NZ, 1, HALF_BLOCKS * NRANDOM)).reshape(-1)
    table = address(jnp.concatenate([mine, global_ids]))
    projected = attention_call(
        table,
        queries.reshape(SHARD_BLOCKS, BLOCK, width),
        keys_values.reshape(2, SHARD_BLOCKS, BLOCK, width),
        out_weight.reshape(-1, BLOCK, out_weight.shape[1]),
    )
    return projected.reshape(ROWS, -1)


def solution(mesh):
    in_specs = (P("seq", "head"), P(None, "seq", "head"), P(), P(), P(None, "head"))
    return jax.shard_map(body, mesh=mesh, in_specs=in_specs, out_specs=P("seq", "head"), check_vma=False)
```

```python
import math

import jax
import jax.numpy as jnp
from jax import lax
from jax.experimental import pallas as pl
from jax.experimental.pallas import tpu as pltpu
from jax.sharding import PartitionSpec as P

HEAD_DIM = 128
BLOCK = 64
NGLOBAL = 2
NRANDOM = 3
MESH = pl.DeviceIdType.MESH

NXH, NY, NZ, NXL, NC = 2, 4, 8, 2, 2
LINES = NXH * NY
SHARD_BLOCKS = 24
ROWS = SHARD_BLOCKS * BLOCK
HALF_BLOCKS = SHARD_BLOCKS // NC
HALF = HALF_BLOCKS * BLOCK
LINE_BLOCKS = NZ * SHARD_BLOCKS
Q_BLOCKS = NZ * HALF_BLOCKS


def coords():
    seq = lax.axis_index("seq")
    head = lax.axis_index("head")
    return seq // (NY * NZ), (seq // NZ) % NY, seq % NZ, head // NC, head % NC


def device(xh, y, z, xl, c):
    return ((xh * NY + y) * NZ + z, xl * NC + c)


def remote(src, dst, send_sem, recv_sem, target):
    return pltpu.make_async_remote_copy(
        src_ref=src, dst_ref=dst, send_sem=send_sem, recv_sem=recv_sem,
        device_id=target, device_id_type=MESH,
    )


def nearest(k):
    return (k % 2) * ((k + 1) // 2) - (1 - k % 2) * (k // 2)


X0, U1, D1, U2, D2, FU, FD, YU, YD, F2, G2, YO = range(12)
NCLASS = 12
FROM_X = (7, 6)
Z_LEAD = 2
ITEMS = 2 * NZ
CHUNK = 3
PARTS = NZ * HALF_BLOCKS // CHUNK
FORWARD = 8
RELAY = 8
LAG = 9
WEIGHT_AT = 512
DELAY = (0, 0, 2, 4, 6)
SCORES_FROM = NZ + DELAY[4]
SCALE = math.log2(math.e) / HEAD_DIM**0.5


def address(block):
    shard, offset = block // SHARD_BLOCKS, block % SHARD_BLOCKS
    line, plane = shard // NZ, shard % NZ
    return ((line * NC + offset // HALF_BLOCKS) * NZ + plane) * HALF_BLOCKS + offset % HALF_BLOCKS


def attention_kernel(
    table, q_ref, kv_ref, w_ref, out_ref, kbuf, vbuf, qbuf, pbuf, obuf,
    zs, zr, cs, cr, bs, br, rzs, rzr, ras, rar, ws, os, ready,
):
    xh, y, z, xl, c = coords()
    line = xh * NY + y
    up, down, opp = (y + 1) % NY, (y + NY - 1) % NY, (y + 2) % NY
    ox = 1 - xh
    to_x, to_up, to_down = device(ox, y, z, xl, c), device(xh, up, z, xl, c), device(xh, down, z, xl, c)
    to_sib, to_lo = device(xh, y, z, xl, 1 - c), device(xh, y, z, 1 - xl, c)
    bufs = (kbuf, vbuf)

    barrier = pltpu.get_barrier_semaphore()
    friends = [
        device(xh, y, (z + dz) % NZ, xl, (c + dc) % NC)
        for dz in range(NZ) for dc in range(NC) if dz or dc
    ] + [to_x, to_up, to_down, to_lo]
    for friend in friends:
        pl.semaphore_signal(barrier, inc=1, device_id=friend, device_id_type=MESH)
    pl.semaphore_wait(barrier, len(friends))

    def piece(kv, ln, half, p):
        return bufs[kv].at[pl.ds(((ln * NC + half) * NZ + p) * HALF_BLOCKS, HALF_BLOCKS)]

    def near_plane(k):
        return (z + nearest(k) + NZ) % NZ

    def z_parts(t, kind, half):
        cols = pl.ds(pl.multiple_of((t - 4 * c) * HEAD_DIM, HEAD_DIM), HEAD_DIM)
        rows = pl.ds(half * HALF_BLOCKS, HALF_BLOCKS)
        if kind == 2:
            return q_ref.at[rows, :, cols], qbuf.at[pl.ds(z * HALF_BLOCKS, HALF_BLOCKS)]
        return kv_ref.at[kind, rows, :, cols], piece(kind, line, half, z)

    def z_each(k, kind, remote_fn, local_fn):
        t = near_plane(k)

        @pl.when(t // 4 == c)
        def _():
            for half in range(NC):
                src, dst = z_parts(t, kind, half)
                mine = jnp.logical_and(t == z, c == half)
                if local_fn is not None:
                    @pl.when(mine)
                    def _():
                        local_fn(pltpu.make_async_copy(src, dst, zr.at[kind, z]))

                @pl.when(jnp.logical_not(mine))
                def _():
                    remote_fn(remote(src, dst, zs.at[kind, half, k], zr.at[kind, z], device(xh, y, t, xl, half)))

    def z_start(k, kind):
        z_each(k, kind, lambda d: d.start(), lambda d: d.start())

    @pl.loop(0, Z_LEAD)
    def _(k):
        z_start(k, 0)

    H = HALF_BLOCKS // 2

    def at(xx, yy):
        return xx * NY + yy

    def routes(kv):
        m = FROM_X[kv]
        h = (m + 1) // 2
        rest = (m, HALF_BLOCKS - m)
        return {
            X0: (line, to_x, (0, HALF_BLOCKS), at(ox, y)),
            U1: (line, to_up, (0, HALF_BLOCKS), at(xh, down)),
            D1: (line, to_down, (0, HALF_BLOCKS), at(xh, up)),
            U2: (at(ox, y), to_up, (0, m), at(ox, down)),
            D2: (at(ox, y), to_down, (0, m), at(ox, up)),
            FU: (at(xh, down), to_up, (0, H), at(xh, opp)),
            FD: (at(xh, up), to_down, (H, H), at(xh, opp)),
            YU: (at(xh, down), to_x, rest, at(ox, down)),
            YD: (at(xh, up), to_x, rest, at(ox, up)),
            F2: (at(ox, down), to_up, (0, h), at(ox, opp)),
            G2: (at(ox, up), to_down, (h, m - h), at(ox, opp)),
            YO: (at(xh, opp), to_x, rest, at(ox, opp)),
        }

    def copy(cls, e, p, kv, ln, target, span):
        ref = piece(kv, ln, c, p).at[pl.ds(*span)]
        return remote(ref, ref, cs.at[cls, e], cr.at[cls, e], target)

    def sib(e, p, kv, ln, half):
        ref = piece(kv, ln, half, p)
        return remote(ref, ref, bs.at[e, ln], br.at[e, ln], to_sib)

    def stages(kv, k, p, stage):
        e = kv * NZ + k
        classes = routes(kv)

        def send(*names):
            for cls in names:
                ln, target, span, _ = classes[cls]
                copy(cls, e, p, kv, ln, target, span).start()

        def wait(*names):
            for cls in names:
                _, target, span, ln = classes[cls]
                copy(cls, e, p, kv, ln, target, span).wait_recv()

        def share(*lines):
            for ln in lines:
                sib(e, p, kv, ln, c).start()

        if stage == 1:
            ref = piece(kv, line, c, p)
            remote(ref, ref, zs.at[kv, 0, 0], zr.at[kv, p], to_x).wait_recv()
            send(X0, U1, D1)
            share(line)
        elif stage == 2:
            wait(X0)
            send(U2, D2)
            wait(U1)
            send(YU, FU)
            wait(D1)
            send(YD, FD)
            share(at(ox, y), at(xh, down), at(xh, up))
        elif stage == 3:
            wait(U2)
            send(F2)
            wait(D2)
            send(G2)
            wait(FU, FD)
            send(YO)
            share(at(xh, opp))
        else:
            wait(YU, YD)
            share(at(ox, down), at(ox, up))
            wait(F2, G2, YO)
            share(at(ox, opp))

    def sib_received(kv):
        @pl.loop(0, NZ)
        def _(k):
            p = near_plane(k)

            @pl.loop(0, LINES)
            def _(ln):
                sib(kv * NZ + k, p, kv, ln, 1 - c).wait_recv()

    column = lax.broadcasted_iota(jnp.int32, (1, 512), 1)
    globals_at = Q_BLOCKS * NRANDOM

    def listed(buf, n, block):
        last_block = LINES * LINE_BLOCKS - 1
        spots = [
            address(jnp.maximum(block - 1, 0)), address(block), address(jnp.minimum(block + 1, last_block)),
        ] + [table[n * NRANDOM + r] for r in range(NRANDOM)] + [table[globals_at + g] for g in range(NGLOBAL)]
        return jnp.concatenate([buf[s] for s in spots], axis=0)

    def doc_block(plane, o):
        return line * LINE_BLOCKS + plane * SHARD_BLOCKS + c * HALF_BLOCKS + o

    def weigh(plane, o):
        n, block = plane * HALF_BLOCKS + o, doc_block(plane, o)
        first = jnp.logical_and(block == 0, column < BLOCK)
        last = jnp.logical_and(
            block == LINES * LINE_BLOCKS - 1, jnp.logical_and(column >= 2 * BLOCK, column < 3 * BLOCK)
        )
        bias = jnp.where(jnp.logical_or(first, last), -jnp.inf, 0.0).astype(jnp.float32)
        scores = lax.dot_general(
            qbuf[n], listed(kbuf, n, block), (((1,), (1,)), ((), ())), preferred_element_type=jnp.float32
        )
        scores = scores * SCALE + bias
        powers = jnp.exp2(scores - jnp.max(scores, axis=1, keepdims=True))
        pbuf[n] = (powers * (1.0 / jnp.sum(powers, axis=1, keepdims=True))).astype(jnp.bfloat16)

    def mix(plane, o):
        n, block = plane * HALF_BLOCKS + o, doc_block(plane, o)
        mixed = jnp.dot(pbuf[n], listed(vbuf, n, block), preferred_element_type=jnp.float32)
        obuf[n] = mixed.astype(jnp.bfloat16)

    def weight_copy(g):
        cols = pl.ds(pl.multiple_of(g * HEAD_DIM, HEAD_DIM), HEAD_DIM)
        return pltpu.make_async_copy(w_ref.at[:, :, cols], kbuf.at[pl.ds(WEIGHT_AT + g * 32, 32)], ws.at[g])

    writers = [device(xh, y, (z + dz) % NZ, xl, c) for dz in range(1, NZ)] + [to_lo, to_sib]

    def sends_done(kv):
        @pl.loop(0, NZ)
        def _(k):
            p = near_plane(k)
            e = kv * NZ + k
            for cls, (ln, target, span, _) in routes(kv).items():
                copy(cls, e, p, kv, ln, target, span).wait_send()

            @pl.loop(0, LINES)
            def _(ln):
                sib(e, p, kv, ln, c).wait_send()

    def blocks_of(plane, fn):
        @pl.loop(0, HALF_BLOCKS // 4)
        def _(m):
            for u in range(4):
                fn(plane, m * 4 + u)

    @pl.loop(0, ITEMS + DELAY[4])
    def _(step):
        for kind, lag in ((0, -Z_LEAD), (1, 5), (2, 6)):
            @pl.when(jnp.logical_and(step >= max(lag, 0), step < NZ + lag))
            def _():
                z_start(step - lag, kind)

        for stage in (4, 3, 2, 1):
            e = step - DELAY[stage]
            for kv in range(2):
                @pl.when(jnp.logical_and(e >= kv * NZ, e < (kv + 1) * NZ))
                def _():
                    k = e - kv * NZ
                    p = near_plane(k)
                    stages(kv, k, p, stage)

        @pl.when(step == SCORES_FROM)
        def _():
            sib_received(0)

            @pl.loop(0, NZ)
            def _(p):
                ref = qbuf.at[pl.ds(p * HALF_BLOCKS, HALF_BLOCKS)]
                remote(ref, ref, zs.at[2, 0, 0], zr.at[2, p], to_x).wait_recv()

        @pl.when(jnp.logical_and(step >= SCORES_FROM, step < SCORES_FROM + NZ // 2))
        def _():
            for u in range(2):
                blocks_of(2 * (step - SCORES_FROM) + u, weigh)

        @pl.when(step == SCORES_FROM + NZ // 2)
        def _():
            sends_done(0)

            @pl.loop(0, NZ)
            def _(g):
                weight_copy(g).start()

            for writer in writers:
                pl.semaphore_signal(ready, inc=1, device_id=writer, device_id_type=MESH)

    sib_received(1)

    def place(half, side, plane, r):
        return kbuf.at[pl.ds((side * NZ + plane) * SHARD_BLOCKS + half * HALF_BLOCKS + r * CHUNK, CHUNK)]

    def rows_of(p, r):
        return obuf.at[pl.ds(p * HALF_BLOCKS + r * CHUNK, CHUNK)]

    def home(r, k, p):
        return remote(rows_of(p, r), place(c, xl, z, r), rzs.at[r, k], rzr.at[r, z], device(xh, y, p, xl, c))

    def onward(cls, i, half, side, p, r, target):
        ref = place(half, side, p, r)
        return remote(ref, ref, ras.at[cls, i], rar.at[cls, i], target)

    pl.semaphore_wait(ready, len(writers))

    def project(r, half, side):
        for w in range(2):
            total = jnp.zeros((CHUNK * BLOCK, 256), jnp.float32)
            for pair in range(NZ):
                left = [
                    kbuf[pl.ds((2 * pair + i) * SHARD_BLOCKS + half * HALF_BLOCKS + r * CHUNK, CHUNK)]
                    for i in range(2)
                ]
                right = [kbuf[pl.ds(WEIGHT_AT + ((side * 2 + w) * 2 + i) * 32 + pair * 4, 4)] for i in range(2)]
                total = total + jnp.dot(
                    jnp.concatenate([v.reshape(CHUNK * BLOCK, HEAD_DIM) for v in left], axis=1),
                    jnp.concatenate([v.reshape(256, HEAD_DIM) for v in right], axis=1),
                    preferred_element_type=jnp.float32,
                )
            result = total.astype(jnp.bfloat16)
            for u in range(CHUNK):
                pbuf[tile(r, half, side) + u, :, w * 256:(w + 1) * 256] = result[u * BLOCK:(u + 1) * BLOCK]

    def tile(r, half, side):
        return (half * 2 + side) * HALF_BLOCKS + r * CHUNK

    def result_copy(r, half, side):
        cols = pl.ds(pl.multiple_of(side * 512, 512), 512)
        return pltpu.make_async_copy(
            pbuf.at[pl.ds(tile(r, half, side), CHUNK)],
            out_ref.at[pl.ds(half * HALF_BLOCKS + r * CHUNK, CHUNK), :, cols],
            os.at[r, half * 2 + side],
        )

    @pl.loop(0, PARTS + FORWARD + LAG + NZ)
    def _(tick):
        @pl.when(tick < PARTS)
        def _():
            r, k = tick // NZ, tick % NZ
            p = near_plane(k)
            for u in range(CHUNK):
                mix(p, r * CHUNK + u)

            @pl.when(k == 0)
            def _():
                pltpu.make_async_copy(rows_of(z, r), place(c, xl, z, r), rzr.at[r, z]).start()

            @pl.when(k > 0)
            def _():
                home(r, k, p).start()

        step = tick - FORWARD

        @pl.when(jnp.logical_and(step >= 0, step < PARTS))
        def _():
            r, k = step // NZ, step % NZ
            p = near_plane(k)
            ref = place(c, xl, p, r)
            remote(ref, ref, rzs.at[0, 0], rzr.at[r, p], to_lo).wait_recv()
            onward(0, step, c, xl, p, r, to_lo).start()
            onward(1, step, c, xl, p, r, to_sib).start()

        @pl.when(jnp.logical_and(step >= RELAY, step < PARTS + RELAY))
        def _():
            i = step - RELAY
            r, p = i // NZ, near_plane(i % NZ)
            onward(0, i, c, 1 - xl, p, r, to_lo).wait_recv()
            onward(2, i, c, 1 - xl, p, r, to_sib).start()

        done = step - LAG - NZ

        @pl.when(jnp.logical_and(done >= 0, done % NZ == 0))
        def _():
            @pl.when(done == 0)
            def _():
                @pl.loop(0, NZ)
                def _(g):
                    weight_copy(g).wait()

            @pl.loop(0, NZ)
            def _(k):
                p = near_plane(k)
                onward(1, done + k, 1 - c, xl, p, done // NZ, to_sib).wait_recv()
                onward(2, done + k, 1 - c, 1 - xl, p, done // NZ, to_sib).wait_recv()

        @pl.when(jnp.logical_and(done >= 0, done % 2 == 0))
        def _():
            r, part = done // NZ, (done % NZ) // 2
            project(r, part // 2, part % 2)
            result_copy(r, part // 2, part % 2).start()

    @pl.loop(0, PARTS)
    def _(i):
        r, k = i // NZ, i % NZ
        p = near_plane(k)

        @pl.when(k > 0)
        def _():
            home(r, k, p).wait_send()

        onward(0, i, c, xl, p, r, to_lo).wait_send()
        onward(1, i, c, xl, p, r, to_sib).wait_send()
        onward(2, i, c, 1 - xl, p, r, to_sib).wait_send()

    sends_done(1)

    @pl.loop(0, NZ)
    def _(k):
        for kind in range(3):
            z_each(k, kind, lambda d: d.wait_send(), None)

    for r in range(HALF_BLOCKS // CHUNK):
        for part in range(4):
            result_copy(r, part // 2, part % 2).wait()


def attention_call(table, queries, keys_values, weight):
    anyspace = pl.BlockSpec(memory_space=pl.ANY)
    dma = pltpu.SemaphoreType.DMA
    key_blocks = LINES * LINE_BLOCKS
    return pl.pallas_call(
        attention_kernel,
        out_shape=jax.ShapeDtypeStruct((SHARD_BLOCKS, BLOCK, weight.shape[-1]), jnp.bfloat16),
        in_specs=[pl.BlockSpec(memory_space=pltpu.SMEM), anyspace, anyspace, anyspace],
        out_specs=anyspace,
        scratch_shapes=[
            pltpu.VMEM((key_blocks, BLOCK, HEAD_DIM), jnp.bfloat16),
            pltpu.VMEM((key_blocks, BLOCK, HEAD_DIM), jnp.bfloat16),
            pltpu.VMEM((Q_BLOCKS, BLOCK, HEAD_DIM), jnp.bfloat16),
            pltpu.VMEM((Q_BLOCKS, BLOCK, 512), jnp.bfloat16),
            pltpu.VMEM((Q_BLOCKS, BLOCK, HEAD_DIM), jnp.bfloat16),
            dma((3, NC, NZ)), dma((3, NZ)),
            dma((NCLASS, ITEMS)), dma((NCLASS, ITEMS)),
            dma((ITEMS, LINES)), dma((ITEMS, LINES)),
            dma((HALF_BLOCKS // CHUNK, NZ)), dma((HALF_BLOCKS // CHUNK, NZ)), dma((3, PARTS)), dma((3, PARTS)),
            dma((NZ,)), dma((HALF_BLOCKS // CHUNK, 4)), pltpu.SemaphoreType.REGULAR,
        ],
        compiler_params=pltpu.CompilerParams(
            collective_id=1, has_side_effects=True, vmem_limit_bytes=60 * 1024 * 1024
        ),
        name="block_attention",
    )(table, queries, keys_values, weight)


def body(queries, keys_values, global_ids, rand_ids, out_weight):
    xh, y, z, xl, c = coords()
    width = queries.shape[1]
    lists = rand_ids.reshape(LINES, NZ, NC, HALF_BLOCKS * NRANDOM)
    mine = lax.dynamic_slice(lists, (xh * NY + y, 0, c, 0), (1, NZ, 1, HALF_BLOCKS * NRANDOM)).reshape(-1)
    table = address(jnp.concatenate([mine, global_ids]))
    projected = attention_call(
        table,
        queries.reshape(SHARD_BLOCKS, BLOCK, width),
        keys_values.reshape(2, SHARD_BLOCKS, BLOCK, width),
        out_weight.reshape(-1, BLOCK, out_weight.shape[1]),
    )
    return projected.reshape(ROWS, -1)


def solution(mesh):
    in_specs = (P("seq", "head"), P(None, "seq", "head"), P(), P(), P(None, "head"))
    return jax.shard_map(body, mesh=mesh, in_specs=in_specs, out_specs=P("seq", "head"), check_vma=False)
```
